256 devices in a mesh: grp: 32 (over y, x, core), mem: 8 (over z).
Axes of the slice: x: 4, y: 4, z: 8, core: 2. Of those that a mesh axis runs over, the one named last changes fastest.
Arguments:
- voxels: bfloat16 [32768, 6, 6, 384], P(('grp', 'mem')), may hold values from -6 to 6
- conv_weight: bfloat16 [3, 3, 3, 64, 64], replicated, may hold values from -0.15625 to 0.15625
- conv_bias: float32 [64], replicated, may hold values from -3 to 3
- row_counts: int32 [256], P(('grp', 'mem')), may hold values from 512 to 2048, as said below
- sample_patch: int32 [524288], P(('grp', 'mem')), may hold values from 0 to 31
- targets: float32 [524288], P(('grp', 'mem')), may hold values from -6 to 6
- query_patch: int32 [16384], P(('grp', 'mem')), may hold values from 0 to 127
Outputs:
- post_var: float32 [32, 8, 2048], P('grp', 'mem')
- post_mean: float32 [32, 8, 2048], P('grp', 'mem')
The draws below stay inside these ranges and needn't reach their ends.
Inputs may be any that keep to these rules, and one draw needn't show every extreme that they name: row_counts[d] is the number of live leading rows of device d; some device has all 2048 rows live.
All inputs are finite; a program needn't handle non-finite values.
Results may differ from the reference program's by a relative error of at most 0.0052.
Values may be sent and summed in bfloat16 or wider, within the bound.
A program may use at most 64 MiB of HBM per device.

```python
import math
import jax
import jax.numpy as jnp
import numpy as np
from jax import lax

C = 64
EDGE = 6
PATCH_DEV = 128
ROWS_DEV = 2048
Q_DEV = 64
F = 512
NDEV = 256
PATCHES = 32768
ROWS = 524288
QUERIES = 16384
QG = 2048
N_GRP = 32
N_MEM = 8


def draw_row_counts(key, part):
    first_key, second_key = jax.random.split(jax.random.fold_in(key, 7))
    counts = jax.random.randint(first_key, (NDEV,), ROWS_DEV // 4, ROWS_DEV + 1)
    chosen = jax.random.randint(second_key, (), 0, NDEV)
    return jnp.where(jnp.arange(NDEV, dtype=jnp.int32) == chosen, ROWS_DEV, counts).astype(jnp.int32)


def touch_ends(result, key, low, largest):
    shape = result.shape
    place = [jax.random.randint(jax.random.fold_in(key, axis), (), 0, shape[axis]) for axis in range(len(shape))]
    result = result.at[tuple(place)].set(low)
    longest = shape.index(max(shape))
    place[longest] = (place[longest] + 1) % shape[longest]
    return result.at[tuple(place)].set(largest)


def shard_levels(key, dims, shards, least, top_value):
    factor_of, own = 1.0, jax.random.fold_in(key, 6)
    for axis_at, parts in shards:
        steps = jnp.exp(jax.random.uniform(jax.random.fold_in(own, axis_at), (parts,), jnp.float32, least / len(shards), top_value / len(shards)))
        factor_of = factor_of * jnp.repeat(steps, dims[axis_at] // parts).reshape([-1 if axis == axis_at else 1 for axis in range(len(dims))])
    return factor_of


def rank_bounds(amount, slope):
    loads = [(1 << 20) // math.isqrt(standing ** slope) + 1 for standing in range(1, amount + 1)]
    spread = 1 + sum(loads) // (1 << 30)
    return np.cumsum(np.array([max(1, weight // spread) for weight in loads]))


def skewed_ids(own_key, shape, amount, slope):
    listing = rank_bounds(amount, slope)
    lot = jax.random.randint(jax.random.fold_in(own_key, 1), shape, 0, int(listing[amount - 1]))
    rank = jnp.searchsorted(jnp.asarray(listing, jnp.int32), lot, side="right")
    return jax.random.permutation(jax.random.fold_in(own_key, 2), amount)[rank].astype(jnp.int32)


def scatter_about(key, dims, width, most, cuts=(), kind=jnp.bfloat16):
    values = jax.random.normal(key, dims, jnp.float32) * width
    if len(cuts) > 0:
        values = shard_levels(key, dims, cuts, -0.22, 0.18) * values
    return jnp.clip(values, min=-most, max=most).astype(kind)


def setup_inputs(seed: int = 0) -> dict:
    splits = jax.random.split(jax.random.key(seed), 8)
    voxels = scatter_about(splits[0], (PATCHES, EDGE, EDGE, EDGE * C), 1.0, 6.0, ((0, 256),))
    conv_weight = scatter_about(splits[1], (3, 3, 3, C, C), (27 * C) ** -0.5, 0.15625)
    conv_bias = scatter_about(splits[2], (C,), 0.5, 3.0, (), jnp.float32)
    row_counts = draw_row_counts(jax.random.fold_in(splits[7], 71), 0)
    sample_patch = touch_ends(skewed_ids(splits[4], (ROWS,), PATCH_DEV // 4, 2), jax.random.fold_in(splits[4], 3), 0, (PATCH_DEV // 4) - 1).astype(jnp.int32)
    targets = scatter_about(splits[5], (ROWS,), 1.0, 6.0, ((0, 256),), jnp.float32)
    query_patch = touch_ends(jax.random.randint(splits[6], (QUERIES,), 0, PATCH_DEV), jax.random.fold_in(splits[6], 1), 0, PATCH_DEV - 1).astype(jnp.int32)
    return {"voxels": voxels, "conv_weight": conv_weight, "conv_bias": conv_bias, "row_counts": row_counts, "sample_patch": sample_patch, "targets": targets, "query_patch": query_patch}


noise_scale = 8.0

def tri_solve(lower, rhs, transposed):
    return lax.linalg.triangular_solve(lower, rhs, left_side=True, lower=True, transpose_a=transposed)

def features_of(volume, conv_weight, conv_bias):
    patch_count = volume.shape[0]
    shaped = volume.reshape(patch_count, EDGE, EDGE, EDGE, C)
    convolved = lax.conv_general_dilated(shaped, conv_weight, (1, 1, 1), 'VALID', dimension_numbers=('NDHWC', 'DHWIO', 'NDHWC'), preferred_element_type=jnp.float32)
    activated = jnp.tanh(convolved + conv_bias).reshape(patch_count, 2, 2, 2, 2, 2, 2, C)
    pooled = jnp.mean(activated, axis=(2, 4, 6))
    return pooled.reshape(patch_count, 8 * C)

def hit_sums(patch_ids, target_part, live_count, patch_count):
    row_total = patch_ids.shape[0]
    live_mask = (jnp.arange(row_total, dtype=jnp.int32) < live_count).astype(jnp.float32)
    onehot = (jnp.arange(patch_count, dtype=jnp.int32)[:, None] == patch_ids[None, :]).astype(jnp.float32)
    paired = jnp.stack([live_mask, live_mask * target_part])
    summed = jnp.einsum('pr,kr->kp', onehot, paired, precision=lax.Precision.HIGHEST)
    return (summed[0], summed[1])

def reference(voxels, conv_weight, conv_bias, row_counts, sample_patch, targets, query_patch):
    volumes = voxels.reshape(NDEV, PATCH_DEV, EDGE, EDGE, EDGE * C)
    sample_ids = sample_patch.reshape(NDEV, ROWS_DEV)
    target_rows = targets.reshape(NDEV, ROWS_DEV)
    query_ids = query_patch.reshape(NDEV, Q_DEV)

    def per_device(inputs):
        volume, patch_ids, target_part, query_part, live_count = inputs
        patch_feats = features_of(volume, conv_weight, conv_bias)
        hits, target_sum = hit_sums(patch_ids, target_part, live_count, PATCH_DEV)
        gram_part = jnp.dot((patch_feats * hits[:, None]).T.astype(jnp.float32), patch_feats.astype(jnp.float32), precision=lax.Precision.HIGHEST, preferred_element_type=jnp.float32)
        moment = jnp.dot(target_sum.astype(jnp.float32), patch_feats.astype(jnp.float32), precision=lax.Precision.HIGHEST, preferred_element_type=jnp.float32)
        queries = jnp.take(patch_feats, query_part, axis=0).astype(jnp.bfloat16)
        return (gram_part, moment, queries)
    grams, moments, queries = lax.map(per_device, (volumes, sample_ids, target_rows, query_ids, row_counts))
    group_gram = jnp.sum(grams.reshape(N_GRP, N_MEM, F, F), axis=1)
    group_moment = jnp.sum(moments.reshape(N_GRP, N_MEM, F), axis=1)
    query_all = queries.reshape(N_GRP, N_MEM, Q_DEV, F).transpose(1, 0, 2, 3).reshape(N_MEM * QG, F).astype(jnp.float32)

    def per_group(inputs):
        gram_whole, moment_whole = inputs
        precision_matrix = jnp.eye(F, dtype=jnp.float32) + gram_whole / noise_scale
        lower = jnp.linalg.cholesky(precision_matrix)
        half_solve = tri_solve(lower, (moment_whole / noise_scale)[:, None], False)
        weights = tri_solve(lower, half_solve, True)[:, 0]
        whitened = tri_solve(lower, query_all.T, False)
        variances = jnp.sum(whitened * whitened, axis=0).reshape(N_MEM, QG)
        means = jnp.dot(query_all.astype(jnp.float32), weights.astype(jnp.float32), precision=lax.Precision.HIGHEST, preferred_element_type=jnp.float32).reshape(N_MEM, QG)
        return (variances, means)
    post_var, post_mean = lax.map(per_group, (group_gram, group_moment))
    return (post_var, post_mean)
```

```python
import functools

import jax
import jax.numpy as jnp
from jax import lax
from jax.experimental import pallas as pl
from jax.experimental.pallas import tpu as pltpu
from jax.sharding import PartitionSpec as P

C = 64
EDGE = 6
NP = 128
HIT = 32
F = 512
NQ = 64
FU = F + 128
PAY = 2 * F + 128
MESH = pl.DeviceIdType.MESH
F32 = jnp.float32
BF16 = jnp.bfloat16
HIGHEST = lax.Precision.HIGHEST


def iota(shape, dim):
    return lax.broadcasted_iota(jnp.int32, shape, dim)


def split2(x):
    hi = x.astype(BF16)
    return hi, (x - hi.astype(F32)).astype(BF16)


def dot(a, b, ca=1, cb=0, precision=None):
    return lax.dot_general(
        a, b, (((ca,), (cb,)), ((), ())), precision=precision, preferred_element_type=F32
    )


def banded(conv_weight):
    parts = [
        jnp.pad(conv_weight, ((0, 0), (0, 0), (zo, 3 - zo), (0, 0), (0, 0))) for zo in (0, 2, 1, 3)
    ]
    return jnp.stack(parts, axis=4).reshape(3, 3 * EDGE * C, 4 * C)


def feature_kernel(count, vox, band, bias, ids, targets, qids, pay, qrows, slab, feats, sem):
    copies = [pltpu.make_async_copy(vox.at[x], slab.at[x], sem.at[x]) for x in range(EDGE)]
    for copy in copies:
        copy.start()

    live = iota((HIT, ids.shape[1]), 1) < count[0]
    mine = jnp.logical_and(ids[...] == iota((HIT, ids.shape[1]), 0), live)
    hits = jnp.sum(jnp.where(mine, 1.0, 0.0), axis=1, keepdims=True)
    tsum = jnp.sum(jnp.where(mine, targets[...], 0.0), axis=1, keepdims=True)
    root = jnp.sqrt(hits)
    scaled = jnp.where(hits > 0, tsum / jnp.where(hits > 0, root, 1.0), 0.0)

    waited = 0
    for cx in range(2):
        acc = None
        for dx in range(3):
            while waited < 2 * cx + dx + 2:
                copies[waited].wait()
                waited += 1
            lhs = jnp.concatenate(
                [
                    slab[2 * cx + dx : 2 * cx + dx + 2, dy : dy + 4].reshape(8 * NP, EDGE * C)
                    for dy in range(3)
                ],
                axis=1,
            )
            part = dot(lhs, band[dx])
            acc = part if acc is None else acc + part
        act = jnp.tanh(acc + bias[...]).reshape(2, 2, 2, NP, 4 * C)
        pooled = act[0, :, 0] + act[0, :, 1] + act[1, :, 0] + act[1, :, 1]
        for cy in range(2):
            cell = (pooled[cy, :, : 2 * C] + pooled[cy, :, 2 * C :]) * 0.125
            feats[:, (2 * cx + cy) * 2 * C : (2 * cx + cy + 1) * 2 * C] = cell

    hi, lo = split2(feats[:HIT, :] * root)
    pay[:, :F] = hi
    pay[:, F : 2 * F] = lo
    t1, t2 = split2(scaled)
    t3 = (scaled - t1.astype(F32) - t2.astype(F32)).astype(BF16)
    lane = iota((HIT, 128), 1)
    tail = jnp.where(lane == 0, t1.astype(F32), 0.0)
    tail = jnp.where(lane == 1, t2.astype(F32), tail)
    tail = jnp.where(lane == 2, t3.astype(F32), tail)
    pay[:, 2 * F :] = tail.astype(BF16)
    pick = (iota((NP, NQ), 0) == qids[...]).astype(F32).astype(BF16)
    qrows[...] = dot(pick, feats[...].astype(BF16), 0, 0).astype(BF16)


def features(vox, band, bias, count, ids, targets, qids):
    vmem = pl.BlockSpec(memory_space=pltpu.VMEM)
    return pl.pallas_call(
        feature_kernel,
        out_shape=(
            jax.ShapeDtypeStruct((HIT, PAY), BF16),
            jax.ShapeDtypeStruct((NQ, F), BF16),
        ),
        in_specs=[
            pl.BlockSpec(memory_space=pltpu.SMEM),
            pl.BlockSpec(memory_space=pl.ANY),
            vmem,
            vmem,
            vmem,
            vmem,
            vmem,
        ],
        out_specs=(vmem, vmem),
        scratch_shapes=[
            pltpu.VMEM((EDGE, EDGE, NP, EDGE * C), BF16),
            pltpu.VMEM((NP, F), F32),
            pltpu.SemaphoreType.DMA((EDGE,)),
        ],
        compiler_params=pltpu.CompilerParams(vmem_limit_bytes=48 << 20),
        name="features",
    )(count, vox, band, bias, ids, targets, qids)


def spread(x, shape=(8, 128)):
    return jnp.broadcast_to(x, shape)


def inverse_factor(gram):
    n = HIT
    wide = jnp.concatenate(
        [gram, jnp.where(iota((n, n), 0) == iota((n, n), 1), 1.0, 0.0), jnp.zeros((n, 64), F32)],
        axis=1,
    )
    sub = iota((8, 128), 0)
    rows = [wide[8 * b : 8 * b + 8] for b in range(4)]
    done = []
    for b in range(4):
        cols = [[spread(rows[t][:, 8 * b + c : 8 * b + c + 1]) for c in range(8)] for t in range(b, 4)]
        for j in range(8):
            heads = [spread(cols[0][c][j : j + 1, :]) for c in range(j, 8)]
            inv = 1.0 / heads[0]
            row = spread(rows[b][j : j + 1, :]) * inv
            heads = [h * inv for h in heads]
            for t in range(4 - b):
                below = jnp.where(sub > j, cols[0][j], 0.0) if t == 0 else cols[t][j]
                rows[b + t] = rows[b + t] - below * row
                for c in range(j + 1, 8):
                    cols[t][c] = cols[t][c] - below * heads[c - j]
        diag = cols[0][0]
        for j in range(1, 8):
            diag = jnp.where(sub == j, cols[0][j], diag)
        done.append(rows[b] * lax.rsqrt(diag))
    return jnp.concatenate(done, axis=0)[:, n : 2 * n]


def group_kernel(
    n_mem, pay, qrows, var, mean,
    blocks, queries, t_hi, t_lo, tt_hi, tt_lo, tt_row,
    bsend, brecv, qloc, xsend, xrecv, ysend, yrecv, csend, crecv,
):
    g, m = lax.axis_index("grp"), lax.axis_index("mem")
    core, plane = lax.rem(g, 2), lax.div(g, 2)
    px, py = lax.rem(plane, 4), lax.div(plane, 4)
    right, left = lax.rem(m + 1, n_mem), lax.rem(m + n_mem - 1, n_mem)
    xs = [(py * 4 + lax.rem(px + s, 4)) * 2 + core for s in (1, 2, 3)]
    ys = [(lax.rem(py + s, 4) * 4 + px) * 2 + core for s in (1, 2, 3)]
    other = plane * 2 + (1 - core)

    barrier = pltpu.get_barrier_semaphore()
    for peer in [(g, right), (g, left)] + [(h, m) for h in xs + ys + [other]]:
        pl.semaphore_signal(barrier, inc=1, device_id=peer, device_id_type=MESH)
    pl.semaphore_wait(barrier, 9)

    def remote(src, dst, send, recv, peer):
        return pltpu.make_async_remote_copy(
            src_ref=src, dst_ref=dst, send_sem=send, recv_sem=recv, device_id=peer, device_id_type=MESH
        )

    def pass_on(slot):
        peer = right if slot % 2 else left
        return remote(
            blocks.at[slot], blocks.at[slot + 2], bsend.at[slot + 2], brecv.at[slot + 2], (g, peer)
        )

    hops = {
        1: remote(pay, blocks.at[1], bsend.at[1], brecv.at[1], (g, right)),
        2: remote(pay, blocks.at[2], bsend.at[2], brecv.at[2], (g, left)),
    }
    for slot in (1, 2, 3, 4, 5):
        hops[slot + 2] = pass_on(slot)
    hops[1].start()
    hops[2].start()
    own = pltpu.make_async_copy(qrows, queries.at[plane, core], qloc.at[0])
    own.start()
    along_x = [
        remote(qrows, queries.at[plane, core], xsend.at[i], xrecv.at[i], (xs[i], m)) for i in range(3)
    ]
    line = queries.at[pl.ds(py * 4, 4), core]
    along_y = [remote(line, line, ysend.at[i], yrecv.at[i], (ys[i], m)) for i in range(3)]
    half = queries.at[:, core]
    across = remote(half, half, csend.at[0], crecv.at[0], (other, m))
    for copy in along_x:
        copy.start()

    t_hi[...] = jnp.zeros_like(t_hi)
    t_lo[...] = jnp.zeros_like(t_lo)
    tt_hi[...] = jnp.zeros_like(tt_hi)
    tt_lo[...] = jnp.zeros_like(tt_lo)

    def eliminate(k):
        src = pay if k == 0 else blocks.at[k]
        a_hi, a_lo = src[:, :F], src[:, F : 2 * F]
        tail = src[:, 2 * F :].astype(F32)
        target = tail[:, 0:1] + tail[:, 1:2] + tail[:, 2:3]
        lane = iota((HIT, 128), 1)
        rest = jnp.concatenate(
            [a_hi.astype(F32) + a_lo.astype(F32), jnp.where(lane == 0, target, 0.0)], axis=1
        )
        both = jnp.concatenate([a_hi, a_lo], axis=0)
        gg = dot(both, both, 1, 1)
        gram = gg[:HIT, :HIT] + (gg[:HIT, HIT:] + gg[HIT:, :HIT])
        gram = gram + jnp.where(iota((HIT, HIT), 0) == iota((HIT, HIT), 1), 8.0, 0.0)
        if k > 0:
            width = 128 * ((32 * k + 127) // 128)
            first = dot(both, tt_hi[:F, :width])
            low = first[:HIT] + (first[HIT:] + dot(a_hi, tt_lo[:F, :width]))
            gram = gram - dot(low, low, 1, 1, HIGHEST)
            l_hi, l_lo = split2(low)
            second = dot(jnp.concatenate([l_hi, l_lo], axis=0), t_hi[:width, :])
            rest = rest - (second[:HIT] + (second[HIT:] + dot(l_hi, t_lo[:width, :])))
        inv = inverse_factor(gram)
        rows = dot(inv, rest, 1, 0, HIGHEST)
        r_hi, r_lo = split2(rows)
        t_hi[HIT * k : HIT * (k + 1), :] = r_hi
        t_lo[HIT * k : HIT * (k + 1), :] = r_lo
        cols = rows.T
        c_hi, c_lo = split2(cols)
        tt_hi[:, HIT * k : HIT * (k + 1)] = c_hi
        tt_lo[:, HIT * k : HIT * (k + 1)] = c_lo
        tt_row[:, HIT * k : HIT * (k + 1)] = cols[F : F + 8, :]

    eliminate(0)
    hops[1].wait_recv()
    hops[2].wait_recv()
    hops[3].start()
    hops[4].start()
    own.wait()
    for copy in along_x:
        copy.wait_recv()
    for copy in along_y:
        copy.start()
    eliminate(1)
    eliminate(2)
    hops[3].wait_recv()
    hops[4].wait_recv()
    hops[5].start()
    hops[6].start()
    eliminate(3)
    eliminate(4)
    hops[5].wait_recv()
    hops[6].wait_recv()
    hops[7].start()
    eliminate(5)
    eliminate(6)
    for copy in along_y:
        copy.wait_recv()
    across.start()
    hops[7].wait_recv()
    eliminate(7)
    across.wait_recv()

    y = tt_row[0:1, :]

    def evaluate(i, carry):
        x = queries[pl.ds(4 * i, 4)].reshape(4 * 2 * NQ, F)
        t = dot(x, tt_hi[:F, :]) + dot(x, tt_lo[:F, :])
        xf = x.astype(F32)
        t0, t1 = t[:, :128], t[:, 128:]
        sq = xf * xf
        sv = (sq[:, :128] + sq[:, 128:256]) + (sq[:, 256:384] + sq[:, 384:]) - (t0 * t0 + t1 * t1)
        sm = t0 * y[:, :128] + t1 * y[:, 128:]
        vs, ms = [], []
        for b in range(4):
            vs.append(jnp.sum(sv[128 * b : 128 * b + 128].T, axis=0, keepdims=True))
            ms.append(jnp.sum(sm[128 * b : 128 * b + 128].T, axis=0, keepdims=True))
        var[i] = jnp.concatenate(vs, axis=0)
        mean[i] = jnp.concatenate(ms, axis=0)
        return carry

    lax.fori_loop(0, 4, evaluate, 0)

    for slot in range(1, 8):
        hops[slot].wait_send()
    for copy in along_x + along_y + [across]:
        copy.wait_send()


def group_posterior(n_mem, pay, qrows):
    vmem = pl.BlockSpec(memory_space=pltpu.VMEM)
    dma = pltpu.SemaphoreType.DMA
    out = jax.ShapeDtypeStruct((4, 4, 128), F32)
    return pl.pallas_call(
        functools.partial(group_kernel, n_mem),
        out_shape=(out, out),
        in_specs=[vmem, vmem],
        out_specs=(vmem, vmem),
        scratch_shapes=[
            pltpu.VMEM((n_mem, HIT, PAY), BF16),
            pltpu.VMEM((16, 2, NQ, F), BF16),
            pltpu.VMEM((256, FU), BF16),
            pltpu.VMEM((256, FU), BF16),
            pltpu.VMEM((FU, 256), BF16),
            pltpu.VMEM((FU, 256), BF16),
            pltpu.VMEM((8, 256), F32),
            dma((8,)), dma((8,)), dma((1,)), dma((3,)), dma((3,)), dma((3,)), dma((3,)), dma((1,)), dma((1,)),
        ],
        compiler_params=pltpu.CompilerParams(
            collective_id=0, has_side_effects=True, vmem_limit_bytes=48 << 20
        ),
        name="group_posterior",
    )(pay, qrows)


def on_device(n_mem, voxels, conv_weight, conv_bias, row_counts, sample_patch, targets, query_patch):
    band = banded(conv_weight)
    bias = jnp.tile(conv_bias, 4).reshape(1, 4 * C)
    pay, qrows = features(
        voxels.transpose(1, 2, 0, 3),
        band,
        bias,
        row_counts,
        sample_patch.reshape(1, -1),
        targets.reshape(1, -1),
        query_patch.reshape(1, -1),
    )
    var, mean = group_posterior(n_mem, pay, qrows)
    return var.reshape(1, 1, -1), mean.reshape(1, 1, -1)


def solution(mesh):
    rows = ("grp", "mem")
    in_specs = (P(rows, None, None, None), P(), P(), P(rows), P(rows), P(rows), P(rows))
    out_specs = (P("grp", "mem", None), P("grp", "mem", None))
    return jax.shard_map(
        functools.partial(on_device, mesh.shape["mem"]),
        mesh=mesh,
        in_specs=in_specs,
        out_specs=out_specs,
        check_vma=False,
    )
```

```python
import functools

import jax
import jax.numpy as jnp
from jax import lax
from jax.experimental import pallas as pl
from jax.experimental.pallas import tpu as pltpu
from jax.sharding import PartitionSpec as P

C = 64
EDGE = 6
NP = 128
HIT = 32
F = 512
NQ = 64
FU = F + 128
PAY = 2 * F + 128
MESH = pl.DeviceIdType.MESH
F32 = jnp.float32
BF16 = jnp.bfloat16
HIGHEST = lax.Precision.HIGHEST


def iota(shape, dim):
    return lax.broadcasted_iota(jnp.int32, shape, dim)


def split2(x):
    hi = x.astype(BF16)
    return hi, (x - hi.astype(F32)).astype(BF16)


def dot(a, b, ca=1, cb=0, precision=None):
    return lax.dot_general(
        a, b, (((ca,), (cb,)), ((), ())), precision=precision, preferred_element_type=F32
    )


def fill_band(weight, band):
    zero = jnp.zeros((C, C), BF16)
    for dx in range(3):
        for dy in range(3):
            taps = [weight[dx, dy, dz] for dz in range(3)]
            at = lambda d: taps[d] if 0 <= d <= 2 else zero
            for zi in range(EDGE):
                row = (dx * 3 + dy) * EDGE * C + zi * C
                band[row : row + C, : 2 * C] = jnp.concatenate([at(zi), at(zi - 2)], axis=1)
                band[row : row + C, 2 * C :] = jnp.concatenate([at(zi - 1), at(zi - 3)], axis=1)


def feature_kernel(
    count, vox, weight, bias, ids, targets, qids, pay, qrows, slab, taps, band, feats, sem, wsem
):
    copies = [pltpu.make_async_copy(vox.at[x], slab.at[x], sem.at[x]) for x in range(EDGE)]
    taps_in = pltpu.make_async_copy(weight, taps, wsem.at[0])
    taps_in.start()
    for copy in copies:
        copy.start()

    live = iota((HIT, ids.shape[1]), 1) < count[0]
    mine = jnp.logical_and(ids[...] == iota((HIT, ids.shape[1]), 0), live)
    hits = jnp.sum(jnp.where(mine, 1.0, 0.0), axis=1, keepdims=True)
    tsum = jnp.sum(jnp.where(mine, targets[...], 0.0), axis=1, keepdims=True)
    root = jnp.sqrt(hits)
    scaled = jnp.where(hits > 0, tsum / jnp.where(hits > 0, root, 1.0), 0.0)
    t1, t2 = split2(scaled)
    t3 = (scaled - t1.astype(F32) - t2.astype(F32)).astype(BF16)
    lane = iota((HIT, 128), 1)
    tail = jnp.where(lane == 0, t1.astype(F32), 0.0)
    tail = jnp.where(lane == 1, t2.astype(F32), tail)
    tail = jnp.where(lane == 2, t3.astype(F32), tail)
    pay[:, 2 * F :] = tail.astype(BF16)

    taps_in.wait()
    fill_band(taps, band)
    shift = jnp.concatenate([bias[...]] * 4, axis=1)
    waited = 0
    for cx in range(2):
        while waited < 2 * cx + 4:
            copies[waited].wait()
            waited += 1
        for cy in range(2):
            lhs = jnp.concatenate(
                [
                    slab[2 * cx + dx : 2 * cx + dx + 2, 2 * cy + dy : 2 * cy + dy + 2].reshape(
                        4 * NP, EDGE * C
                    )
                    for dx in range(3)
                    for dy in range(3)
                ],
                axis=1,
            )
            act = jnp.tanh(dot(lhs, band[...]) + shift).reshape(4, NP, 4 * C)
            pooled = (act[0] + act[1]) + (act[2] + act[3])
            cell = (pooled[:, : 2 * C] + pooled[:, 2 * C :]) * 0.125
            feats[:, (2 * cx + cy) * 2 * C : (2 * cx + cy + 1) * 2 * C] = cell

    hi, lo = split2(feats[:HIT, :] * root)
    pay[:, :F] = hi
    pay[:, F : 2 * F] = lo
    pick = (iota((NP, NQ), 0) == qids[...]).astype(F32).astype(BF16)
    qrows[...] = dot(pick, feats[...].astype(BF16), 0, 0).astype(BF16)


def features(vox, weight, bias, count, ids, targets, qids):
    vmem, hbm = pl.BlockSpec(memory_space=pltpu.VMEM), pl.BlockSpec(memory_space=pl.ANY)
    return pl.pallas_call(
        feature_kernel,
        out_shape=(
            jax.ShapeDtypeStruct((HIT, PAY), BF16),
            jax.ShapeDtypeStruct((NQ, F), BF16),
        ),
        in_specs=[pl.BlockSpec(memory_space=pltpu.SMEM), hbm, hbm, vmem, vmem, vmem, vmem],
        out_specs=(vmem, vmem),
        scratch_shapes=[
            pltpu.VMEM((EDGE, EDGE, NP, EDGE * C), BF16),
            pltpu.VMEM((3, 3, 3, C, C), BF16),
            pltpu.VMEM((9 * EDGE * C, 4 * C), BF16),
            pltpu.VMEM((NP, F), F32),
            pltpu.SemaphoreType.DMA((EDGE,)),
            pltpu.SemaphoreType.DMA((1,)),
        ],
        compiler_params=pltpu.CompilerParams(vmem_limit_bytes=56 << 20),
        name="features",
    )(count, vox, weight, bias, ids, targets, qids)


def spread(x, shape=(8, 128)):
    return jnp.broadcast_to(x, shape)


def inverse_factor(gram):
    n = gram.shape[0]
    eye = jnp.where(iota((n, n), 0) == iota((n, n), 1), 1.0, 0.0)
    parts = [gram, eye] if n == 64 else [gram, eye, jnp.zeros((n, 128 - 2 * n), F32)]
    wide = jnp.concatenate(parts, axis=1)
    sub = iota((8, 128), 0)
    count = n // 8
    rows = [wide[8 * b : 8 * b + 8] for b in range(count)]
    done = []
    for b in range(count):
        cols = [
            [spread(rows[t][:, 8 * b + c : 8 * b + c + 1]) for c in range(8)] for t in range(b, count)
        ]
        for j in range(8):
            heads = [spread(cols[0][c][j : j + 1, :]) for c in range(j, 8)]
            inv = 1.0 / heads[0]
            row = spread(rows[b][j : j + 1, :]) * inv
            heads = [h * inv for h in heads]
            for t in range(count - b):
                below = jnp.where(sub > j, cols[0][j], 0.0) if t == 0 else cols[t][j]
                rows[b + t] = rows[b + t] - below * row
                for c in range(j + 1, 8):
                    cols[t][c] = cols[t][c] - below * heads[c - j]
        diag = cols[0][0]
        for j in range(1, 8):
            diag = jnp.where(sub == j, cols[0][j], diag)
        done.append(rows[b] * lax.rsqrt(diag))
    return jnp.concatenate(done, axis=0)[:, n : 2 * n]


def eliminate(src, at, first, t_hi, t_lo, tt_hi, tt_lo, tt_row):
    n = src.shape[0]
    a_hi, a_lo = src[:, :F], src[:, F : 2 * F]
    tail = src[:, 2 * F :].astype(F32)
    target = tail[:, 0:1] + tail[:, 1:2] + tail[:, 2:3]
    rest = jnp.concatenate(
        [a_hi.astype(F32) + a_lo.astype(F32), jnp.where(iota((n, 128), 1) == 0, target, 0.0)], axis=1
    )
    both = jnp.concatenate([a_hi, a_lo], axis=0)
    gg = dot(both, both, 1, 1)
    gram = gg[:n, :n] + (gg[:n, n:] + gg[n:, :n])
    gram = gram + jnp.where(iota((n, n), 0) == iota((n, n), 1), 8.0, 0.0)
    if not first:
        part = dot(both, tt_hi[:F, :])
        low = part[:n] + (part[n:] + dot(a_hi, tt_lo[:F, :]))
        gram = gram - dot(low, low, 1, 1, HIGHEST)
        l_hi, l_lo = split2(low)
        part = dot(jnp.concatenate([l_hi, l_lo], axis=0), t_hi[...])
        rest = rest - (part[:n] + (part[n:] + dot(l_hi, t_lo[...])))
    rows = dot(inverse_factor(gram), rest, 1, 0, HIGHEST)
    r_hi, r_lo = split2(rows)
    t_hi[at : at + n, :] = r_hi
    t_lo[at : at + n, :] = r_lo
    cols = rows.T
    c_hi, c_lo = split2(cols)
    tt_hi[:, at : at + n] = c_hi
    tt_lo[:, at : at + n] = c_lo
    tt_row[:, at : at + n] = cols[F : F + 8, :]


def evaluate(queries, tt_hi, tt_lo, tt_row, out):
    y = tt_row[0:1, :]

    def chunk(i, carry):
        x = queries[pl.ds(4 * i, 4)].reshape(4 * 2 * NQ, F)
        t = dot(x, tt_hi[:F, :]) + dot(x, tt_lo[:F, :])
        xf = x.astype(F32)
        t0, t1 = t[:, :128], t[:, 128:]
        sq = xf * xf
        sv = (sq[:, :128] + sq[:, 128:256]) + (sq[:, 256:384] + sq[:, 384:]) - (t0 * t0 + t1 * t1)
        sm = t0 * y[:, :128] + t1 * y[:, 128:]
        for half, part in ((0, sv), (1, sm)):
            lines = [
                jnp.sum(part[128 * b : 128 * b + 128].T, axis=0, keepdims=True) for b in range(4)
            ]
            out[half, i] = jnp.concatenate(lines, axis=0)
        return carry

    lax.fori_loop(0, 4, chunk, 0)


def group_kernel(
    n_mem, pay, qrows, out,
    blocks, queries, t_hi, t_lo, tt_hi, tt_lo, tt_row,
    bsend, brecv, qloc, psend, precv, lsend, lrecv, csend, crecv,
):
    g, m = lax.axis_index("grp"), lax.axis_index("mem")
    core, plane = lax.rem(g, 2), lax.div(g, 2)
    px, py = lax.rem(plane, 4), lax.div(plane, 4)
    right, left = lax.rem(m + 1, n_mem), lax.rem(m + n_mem - 1, n_mem)
    xs = [(py * 4 + lax.rem(px + s, 4)) * 2 + core for s in (1, 2, 3)]
    ys = [(lax.rem(py + s, 4) * 4 + px) * 2 + core for s in (1, 2, 3)]
    other = plane * 2 + (1 - core)

    barrier = pltpu.get_barrier_semaphore()
    for peer in [(g, right), (g, left)] + [(h, m) for h in xs + ys + [other]]:
        pl.semaphore_signal(barrier, inc=1, device_id=peer, device_id_type=MESH)
    pl.semaphore_wait(barrier, 9)

    def remote(src, dst, send, recv, peer):
        return pltpu.make_async_remote_copy(
            src_ref=src, dst_ref=dst, send_sem=send, recv_sem=recv, device_id=peer, device_id_type=MESH
        )

    def pass_on(slot):
        peer = right if slot % 2 else left
        return remote(
            blocks.at[slot], blocks.at[slot + 2], bsend.at[slot + 2], brecv.at[slot + 2], (g, peer)
        )

    hops = {
        1: remote(pay, blocks.at[1], bsend.at[1], brecv.at[1], (g, right)),
        2: remote(pay, blocks.at[2], bsend.at[2], brecv.at[2], (g, left)),
    }
    for slot in (1, 2, 3, 4, 5):
        hops[slot + 2] = pass_on(slot)
    hops[1].start()
    hops[2].start()
    base = pltpu.make_async_copy(pay, blocks.at[0], qloc.at[1])
    base.start()

    half = NQ // 2
    top, bottom = pl.ds(0, half), pl.ds(half, half)
    near = [
        remote(qrows.at[top], queries.at[py, px, core, top], psend.at[i], precv.at[i], (xs[i], m))
        for i in range(3)
    ] + [
        remote(
            qrows.at[bottom], queries.at[py, px, core, bottom], psend.at[3 + i], precv.at[3 + i], (ys[i], m)
        )
        for i in range(3)
    ]
    row, column = queries.at[py, :, core, top], queries.at[:, px, core, bottom]
    far = [remote(row, row, lsend.at[i], lrecv.at[i], (ys[i], m)) for i in range(3)] + [
        remote(column, column, lsend.at[3 + i], lrecv.at[3 + i], (xs[i], m)) for i in range(3)
    ]
    mine = queries.at[:, :, core]
    across = remote(mine, mine, csend.at[0], crecv.at[0], (other, m))
    own = pltpu.make_async_copy(qrows, queries.at[py, px, core], qloc.at[0])
    for copy in near:
        copy.start()
    own.start()

    factor = (t_hi, t_lo, tt_hi, tt_lo, tt_row)
    for ref in factor:
        ref[...] = jnp.zeros_like(ref)

    base.wait()
    eliminate(blocks[0], 192, True, *factor)
    hops[1].wait_recv()
    hops[2].wait_recv()
    hops[3].start()
    hops[4].start()
    own.wait()
    for copy in near:
        copy.wait_recv()
    for copy in far:
        copy.start()
    eliminate(blocks[1:3].reshape(2 * HIT, PAY), 0, False, *factor)
    hops[3].wait_recv()
    hops[4].wait_recv()
    hops[5].start()
    hops[6].start()
    eliminate(blocks[3:5].reshape(2 * HIT, PAY), 64, False, *factor)
    hops[5].wait_recv()
    hops[6].wait_recv()
    hops[7].start()
    eliminate(blocks[5:7].reshape(2 * HIT, PAY), 128, False, *factor)
    for copy in far:
        copy.wait_recv()
    across.start()
    hops[7].wait_recv()
    eliminate(blocks[7], 224, False, *factor)
    across.wait_recv()
    evaluate(queries.reshape(16, 2, NQ, F), tt_hi, tt_lo, tt_row, out)

    for slot in range(1, 8):
        hops[slot].wait_send()
    for copy in near + far + [across]:
        copy.wait_send()


def group_posterior(n_mem, pay, qrows):
    vmem = pl.BlockSpec(memory_space=pltpu.VMEM)
    dma = pltpu.SemaphoreType.DMA
    return pl.pallas_call(
        functools.partial(group_kernel, n_mem),
        out_shape=jax.ShapeDtypeStruct((2, 4, 4, 128), F32),
        in_specs=[pl.BlockSpec(memory_space=pl.ANY)] * 2,
        out_specs=vmem,
        scratch_shapes=[
            pltpu.VMEM((n_mem, HIT, PAY), BF16),
            pltpu.VMEM((4, 4, 2, NQ, F), BF16),
            pltpu.VMEM((256, FU), BF16),
            pltpu.VMEM((256, FU), BF16),
            pltpu.VMEM((FU, 256), BF16),
            pltpu.VMEM((FU, 256), BF16),
            pltpu.VMEM((8, 256), F32),
            dma((8,)), dma((8,)), dma((2,)), dma((6,)), dma((6,)), dma((6,)), dma((6,)), dma((1,)), dma((1,)),
        ],
        compiler_params=pltpu.CompilerParams(
            collective_id=0, has_side_effects=True, vmem_limit_bytes=48 << 20
        ),
        name="group_posterior",
    )(pay, qrows)


def on_device(n_mem, voxels, conv_weight, conv_bias, row_counts, sample_patch, targets, query_patch):
    pay, qrows = features(
        voxels.transpose(1, 2, 0, 3),
        conv_weight,
        conv_bias.reshape(1, C),
        row_counts,
        sample_patch.reshape(1, -1),
        targets.reshape(1, -1),
        query_patch.reshape(1, -1),
    )
    out = group_posterior(n_mem, pay, qrows)
    return out[0].reshape(1, 1, -1), out[1].reshape(1, 1, -1)


def solution(mesh):
    rows = ("grp", "mem")
    in_specs = (P(rows, None, None, None), P(), P(), P(rows), P(rows), P(rows), P(rows))
    out_specs = (P("grp", "mem", None), P("grp", "mem", None))
    return jax.shard_map(
        functools.partial(on_device, mesh.shape["mem"]),
        mesh=mesh,
        in_specs=in_specs,
        out_specs=out_specs,
        check_vma=False,
    )
```

```python
import functools

import jax
import jax.numpy as jnp
from jax import lax
from jax.experimental import pallas as pl
from jax.experimental.pallas import tpu as pltpu
from jax.sharding import PartitionSpec as P

C = 64
EDGE = 6
NP = 128
HIT = 32
F = 512
NQ = 64
FU = F + 128
TOP = 32767.0
MESH = pl.DeviceIdType.MESH
F32 = jnp.float32
BF16 = jnp.bfloat16
HIGHEST = lax.Precision.HIGHEST


def iota(shape, dim):
    return lax.broadcasted_iota(jnp.int32, shape, dim)


def split2(x):
    hi = x.astype(BF16)
    return hi, (x - hi.astype(F32)).astype(BF16)


def dot(a, b, ca=1, cb=0, precision=None):
    return lax.dot_general(
        a, b, (((ca,), (cb,)), ((), ())), precision=precision, preferred_element_type=F32
    )


def fill_band(weight, band):
    zero = jnp.zeros((C, C), BF16)
    for dx in range(3):
        for dy in range(3):
            taps = [weight[dx, dy, dz] for dz in range(3)]
            at = lambda d: taps[d] if 0 <= d <= 2 else zero
            for zi in range(EDGE):
                row = (dx * 3 + dy) * EDGE * C + zi * C
                band[row : row + C, : 2 * C] = jnp.concatenate([at(zi), at(zi - 2)], axis=1)
                band[row : row + C, 2 * C :] = jnp.concatenate([at(zi - 1), at(zi - 3)], axis=1)


def feature_kernel(
    count, vox, weight, bias, ids, targets, qids, pay, aux, qrows, slab, taps, band, feats, sem, wsem
):
    copies = [pltpu.make_async_copy(vox.at[x], slab.at[x], sem.at[x]) for x in range(EDGE)]
    taps_in = pltpu.make_async_copy(weight, taps, wsem.at[0])
    taps_in.start()
    for copy in copies:
        copy.start()

    live = iota((HIT, ids.shape[1]), 1) < count[0]
    mine = jnp.logical_and(ids[...] == iota((HIT, ids.shape[1]), 0), live)
    hits = jnp.sum(jnp.where(mine, 1.0, 0.0), axis=1, keepdims=True)
    tsum = jnp.sum(jnp.where(mine, targets[...], 0.0), axis=1, keepdims=True)
    root = jnp.sqrt(hits)
    scaled = jnp.where(hits > 0, tsum / jnp.where(hits > 0, root, 1.0), 0.0)
    taps_in.wait()
    fill_band(taps, band)
    shift = jnp.concatenate([bias[...]] * 4, axis=1)
    waited = 0
    for cx in range(2):
        while waited < 2 * cx + 4:
            copies[waited].wait()
            waited += 1
        for cy in range(2):
            lhs = jnp.concatenate(
                [
                    slab[2 * cx + dx : 2 * cx + dx + 2, 2 * cy + dy : 2 * cy + dy + 2].reshape(
                        4 * NP, EDGE * C
                    )
                    for dx in range(3)
                    for dy in range(3)
                ],
                axis=1,
            )
            act = jnp.tanh(dot(lhs, band[...]) + shift).reshape(4, NP, 4 * C)
            pooled = (act[0] + act[1]) + (act[2] + act[3])
            cell = (pooled[:, : 2 * C] + pooled[:, 2 * C :]) * 0.125
            feats[:, (2 * cx + cy) * 2 * C : (2 * cx + cy + 1) * 2 * C] = cell

    rows = feats[:HIT, :]
    peak = jnp.max(jnp.abs(rows), axis=1, keepdims=True)
    unit = jnp.where(peak > 0, TOP / jnp.where(peak > 0, peak, 1.0), 0.0)
    pay[...] = jnp.round(rows * unit).astype(jnp.int32).astype(jnp.int16)
    lane = iota((HIT, 128), 1)
    sides = jnp.where(lane == 0, scaled, jnp.where(lane == 1, peak * (root * (1.0 / TOP)), 0.0))
    aux[...] = jnp.zeros_like(aux)
    aux[:, :HIT] = sides.T[:8, :]
    pick = (iota((NP, NQ), 0) == qids[...]).astype(F32).astype(BF16)
    qrows[...] = dot(pick, feats[...].astype(BF16), 0, 0).astype(BF16)


def features(vox, weight, bias, count, ids, targets, qids):
    vmem, hbm = pl.BlockSpec(memory_space=pltpu.VMEM), pl.BlockSpec(memory_space=pl.ANY)
    return pl.pallas_call(
        feature_kernel,
        out_shape=(
            jax.ShapeDtypeStruct((HIT, F), jnp.int16),
            jax.ShapeDtypeStruct((8, 128), F32),
            jax.ShapeDtypeStruct((NQ, F), BF16),
        ),
        in_specs=[pl.BlockSpec(memory_space=pltpu.SMEM), hbm, hbm, vmem, vmem, vmem, vmem],
        out_specs=(vmem, vmem, vmem),
        scratch_shapes=[
            pltpu.VMEM((EDGE, EDGE, NP, EDGE * C), BF16),
            pltpu.VMEM((3, 3, 3, C, C), BF16),
            pltpu.VMEM((9 * EDGE * C, 4 * C), BF16),
            pltpu.VMEM((NP, F), F32),
            pltpu.SemaphoreType.DMA((EDGE,)),
            pltpu.SemaphoreType.DMA((1,)),
        ],
        compiler_params=pltpu.CompilerParams(vmem_limit_bytes=56 << 20),
        name="features",
    )(count, vox, weight, bias, ids, targets, qids)


def spread(x, shape=(8, 128)):
    return jnp.broadcast_to(x, shape)


def inverse_factor(gram):
    n = gram.shape[0]
    eye = jnp.where(iota((n, n), 0) == iota((n, n), 1), 1.0, 0.0)
    parts = [gram, eye] if n == 64 else [gram, eye, jnp.zeros((n, 128 - 2 * n), F32)]
    wide = jnp.concatenate(parts, axis=1)
    sub = iota((8, 128), 0)
    count = n // 8
    rows = [wide[8 * b : 8 * b + 8] for b in range(count)]
    done = []
    for b in range(count):
        cols = [
            [spread(rows[t][:, 8 * b + c : 8 * b + c + 1]) for c in range(8)] for t in range(b, count)
        ]
        for j in range(8):
            heads = [spread(cols[0][c][j : j + 1, :]) for c in range(j, 8)]
            inv = 1.0 / heads[0]
            row = spread(rows[b][j : j + 1, :]) * inv
            heads = [h * inv for h in heads]
            for t in range(count - b):
                below = jnp.where(sub > j, cols[0][j], 0.0) if t == 0 else cols[t][j]
                rows[b + t] = rows[b + t] - below * row
                for c in range(j + 1, 8):
                    cols[t][c] = cols[t][c] - below * heads[c - j]
        diag = cols[0][0]
        for j in range(1, 8):
            diag = jnp.where(sub == j, cols[0][j], diag)
        done.append(rows[b] * lax.rsqrt(diag))
    return jnp.concatenate(done, axis=0)[:, n : 2 * n]


def eliminate(codes, sides, at, first, t_hi, t_lo, tt_hi, tt_lo, tt_row):
    n = codes.shape[0]
    column = jnp.concatenate([side.T[:HIT] for side in sides], axis=0)
    a_hi, a_lo = split2(codes.astype(jnp.int32).astype(F32) * column[:, 1:2])
    rest = jnp.concatenate(
        [
            a_hi.astype(F32) + a_lo.astype(F32),
            jnp.where(iota((n, 128), 1) == 0, column[:, 0:1], 0.0),
        ],
        axis=1,
    )
    both = jnp.concatenate([a_hi, a_lo], axis=0)
    gg = dot(both, both, 1, 1)
    gram = gg[:n, :n] + (gg[:n, n:] + gg[n:, :n])
    gram = gram + jnp.where(iota((n, n), 0) == iota((n, n), 1), 8.0, 0.0)
    if not first:
        part = dot(both, tt_hi[:F, :])
        low = part[:n] + (part[n:] + dot(a_hi, tt_lo[:F, :]))
        gram = gram - dot(low, low, 1, 1, HIGHEST)
        l_hi, l_lo = split2(low)
        part = dot(jnp.concatenate([l_hi, l_lo], axis=0), t_hi[...])
        rest = rest - (part[:n] + (part[n:] + dot(l_hi, t_lo[...])))
    rows = dot(inverse_factor(gram), rest, 1, 0, HIGHEST)
    r_hi, r_lo = split2(rows)
    t_hi[at : at + n, :] = r_hi
    t_lo[at : at + n, :] = r_lo
    cols = rows.T
    c_hi, c_lo = split2(cols)
    tt_hi[:, at : at + n] = c_hi
    tt_lo[:, at : at + n] = c_lo
    tt_row[:, at : at + n] = cols[F : F + 8, :]


def evaluate(queries, tt_hi, tt_lo, tt_row):
    y = tt_row[0:1, :]
    var, mean = [], []
    for i in range(2):
        x = queries[8 * i : 8 * i + 8].reshape(8 * NQ, F)
        t = dot(x, tt_hi[:F, :]) + dot(x, tt_lo[:F, :])
        xf = x.astype(F32)
        t0, t1 = t[:, :128], t[:, 128:]
        sq = xf * xf
        sv = (sq[:, :128] + sq[:, 128:256]) + (sq[:, 256:384] + sq[:, 384:]) - (t0 * t0 + t1 * t1)
        sm = t0 * y[:, :128] + t1 * y[:, 128:]
        for part, lines in ((sv, var), (sm, mean)):
            for b in range(4):
                lines.append(jnp.sum(part[128 * b : 128 * b + 128].T, axis=0, keepdims=True))
    return jnp.concatenate(var, axis=0), jnp.concatenate(mean, axis=0)


def group_kernel(
    n_mem, pay, aux, qrows, out,
    blocks, sides, queries, t_hi, t_lo, tt_hi, tt_lo, tt_row,
    bsend, brecv, ssend, srecv, qloc, psend, precv, lsend, lrecv, csend, crecv,
):
    g, m = lax.axis_index("grp"), lax.axis_index("mem")
    core, plane = lax.rem(g, 2), lax.div(g, 2)
    px, py = lax.rem(plane, 4), lax.div(plane, 4)
    zs = [lax.rem(m + n_mem + d, n_mem) for d in (1, -1, 2, -2, 3, -3, 4)]
    xs = [(py * 4 + lax.rem(px + s, 4)) * 2 + core for s in (1, 2, 3)]
    ys = [(lax.rem(py + s, 4) * 4 + px) * 2 + core for s in (1, 2, 3)]
    other = plane * 2 + (1 - core)

    barrier = pltpu.get_barrier_semaphore()
    for peer in [(g, z) for z in zs] + [(h, m) for h in xs + ys + [other]]:
        pl.semaphore_signal(barrier, inc=1, device_id=peer, device_id_type=MESH)
    pl.semaphore_wait(barrier, 14)

    def remote(src, dst, send, recv, peer):
        return pltpu.make_async_remote_copy(
            src_ref=src, dst_ref=dst, send_sem=send, recv_sem=recv, device_id=peer, device_id_type=MESH
        )

    hops = []
    for i, z in enumerate(zs):
        hops.append(
            (
                remote(pay, blocks.at[i + 1], bsend.at[i], brecv.at[i], (g, z)),
                remote(aux, sides.at[i + 1], ssend.at[i], srecv.at[i], (g, z)),
            )
        )
    base = (
        pltpu.make_async_copy(pay, blocks.at[0], qloc.at[1]),
        pltpu.make_async_copy(aux, sides.at[0], qloc.at[2]),
    )
    for codes, side in [base] + hops:
        side.start()
        codes.start()

    half = NQ // 2
    top, bottom = pl.ds(0, half), pl.ds(half, half)
    near = [
        remote(qrows.at[top], queries.at[core, py, px, top], psend.at[i], precv.at[i], (xs[i], m))
        for i in range(3)
    ] + [
        remote(
            qrows.at[bottom], queries.at[core, py, px, bottom], psend.at[3 + i], precv.at[3 + i], (ys[i], m)
        )
        for i in range(3)
    ]
    row, column = queries.at[core, py, :, top], queries.at[core, :, px, bottom]
    far = [remote(row, row, lsend.at[i], lrecv.at[i], (ys[i], m)) for i in range(3)] + [
        remote(column, column, lsend.at[3 + i], lrecv.at[3 + i], (xs[i], m)) for i in range(3)
    ]
    mine = queries.at[core]
    across = remote(mine, mine, csend.at[0], crecv.at[0], (other, m))
    own = pltpu.make_async_copy(qrows, queries.at[core, py, px], qloc.at[0])
    for copy in near:
        copy.start()
    own.start()

    factor = (t_hi, t_lo, tt_hi, tt_lo, tt_row)
    for ref in factor:
        ref[...] = jnp.zeros_like(ref)

    def step(slots, at):
        for slot in slots:
            if slot == 0:
                base[0].wait()
                base[1].wait()
            else:
                hops[slot - 1][0].wait_recv()
                hops[slot - 1][1].wait_recv()
        lo, hi = slots[0], slots[-1] + 1
        eliminate(
            blocks[lo:hi].reshape((hi - lo) * HIT, F), [sides[i] for i in slots], at, lo == 0, *factor
        )

    step((0,), 192)
    own.wait()
    for copy in near:
        copy.wait_recv()
    for copy in far:
        copy.start()
    step((1, 2), 0)
    step((3, 4), 64)
    step((5, 6), 128)
    for copy in far:
        copy.wait_recv()
    across.start()
    step((7,), 224)

    def half_lines(which):
        return evaluate(queries.at[which].reshape(16, NQ, F), tt_hi, tt_lo, tt_row)

    near_half = half_lines(core)
    across.wait_recv()
    far_half = half_lines(1 - core)
    for i in range(2):
        even = jnp.where(core == 0, near_half[i], far_half[i])
        odd = jnp.where(core == 0, far_half[i], near_half[i])
        for side in range(2):
            lanes = slice(NQ * side, NQ * (side + 1))
            out[i, :, side, :] = jnp.concatenate([even[:, lanes], odd[:, lanes]], axis=1)

    for codes, side in hops:
        codes.wait_send()
        side.wait_send()
    for copy in near + far + [across]:
        copy.wait_send()


def group_posterior(n_mem, pay, aux, qrows):
    vmem = pl.BlockSpec(memory_space=pltpu.VMEM)
    dma = pltpu.SemaphoreType.DMA
    return pl.pallas_call(
        functools.partial(group_kernel, n_mem),
        out_shape=jax.ShapeDtypeStruct((2, 8, 2, 128), F32),
        in_specs=[pl.BlockSpec(memory_space=pl.ANY)] * 3,
        out_specs=vmem,
        scratch_shapes=[
            pltpu.VMEM((n_mem, HIT, F), jnp.int16),
            pltpu.VMEM((n_mem, 8, 128), F32),
            pltpu.VMEM((2, 4, 4, NQ, F), BF16),
            pltpu.VMEM((256, FU), BF16),
            pltpu.VMEM((256, FU), BF16),
            pltpu.VMEM((FU, 256), BF16),
            pltpu.VMEM((FU, 256), BF16),
            pltpu.VMEM((8, 256), F32),
            dma((7,)), dma((7,)), dma((7,)), dma((7,)), dma((3,)), dma((6,)), dma((6,)), dma((6,)), dma((6,)), dma((1,)), dma((1,)),
        ],
        compiler_params=pltpu.CompilerParams(
            collective_id=0, has_side_effects=True, vmem_limit_bytes=63 << 20
        ),
        name="group_posterior",
    )(pay, aux, qrows)


def on_device(n_mem, voxels, conv_weight, conv_bias, row_counts, sample_patch, targets, query_patch):
    pay, aux, qrows = features(
        voxels.transpose(1, 2, 0, 3),
        conv_weight,
        conv_bias.reshape(1, C),
        row_counts,
        sample_patch.reshape(1, -1),
        targets.reshape(1, -1),
        query_patch.reshape(1, -1),
    )
    out = group_posterior(n_mem, pay, aux, qrows)
    return out[0].reshape(1, 1, -1), out[1].reshape(1, 1, -1)


def solution(mesh):
    rows = ("grp", "mem")
    in_specs = (P(rows, None, None, None), P(), P(), P(rows), P(rows), P(rows), P(rows))
    out_specs = (P("grp", "mem", None), P("grp", "mem", None))
    return jax.shard_map(
        functools.partial(on_device, mesh.shape["mem"]),
        mesh=mesh,
        in_specs=in_specs,
        out_specs=out_specs,
        check_vma=False,
    )
```

```python
import functools

import jax
import jax.numpy as jnp
from jax import lax
from jax.experimental import pallas as pl
from jax.experimental.pallas import tpu as pltpu
from jax.sharding import PartitionSpec as P

C = 64
EDGE = 6
NP = 128
HIT = 32
F = 512
NQ = 64
FU = F + 128
TOP = 32767.0
MESH = pl.DeviceIdType.MESH
F32 = jnp.float32
BF16 = jnp.bfloat16
HIGHEST = lax.Precision.HIGHEST


def iota(shape, dim):
    return lax.broadcasted_iota(jnp.int32, shape, dim)


def split2(x):
    hi = x.astype(BF16)
    return hi, (x - hi.astype(F32)).astype(BF16)


def dot(a, b, ca=1, cb=0, precision=None):
    return lax.dot_general(
        a, b, (((ca,), (cb,)), ((), ())), precision=precision, preferred_element_type=F32
    )


def fill_band(weight, band):
    zero = jnp.zeros((C, C), BF16)
    for dx in range(3):
        for dy in range(3):
            taps = [weight[dx, dy, dz] for dz in range(3)]
            at = lambda d: taps[d] if 0 <= d <= 2 else zero
            for zi in range(EDGE):
                row = (dx * 3 + dy) * EDGE * C + zi * C
                band[row : row + C, : 2 * C] = jnp.concatenate([at(zi), at(zi - 2)], axis=1)
                band[row : row + C, 2 * C :] = jnp.concatenate([at(zi - 1), at(zi - 3)], axis=1)


def features(
    count, vox, weight, bias, ids, targets, qids, pay, aux, qrows, slab, taps, band, feats, sem, wsem
):
    copies = [pltpu.make_async_copy(vox.at[x], slab.at[x], sem.at[x]) for x in range(EDGE)]
    taps_in = pltpu.make_async_copy(weight, taps, wsem.at[0])
    taps_in.start()
    for copy in copies:
        copy.start()

    live = iota((HIT, ids.shape[1]), 1) < count[0]
    mine = jnp.logical_and(ids[...] == iota((HIT, ids.shape[1]), 0), live)
    hits = jnp.sum(jnp.where(mine, 1.0, 0.0), axis=1, keepdims=True)
    tsum = jnp.sum(jnp.where(mine, targets[...], 0.0), axis=1, keepdims=True)
    root = jnp.sqrt(hits)
    scaled = jnp.where(hits > 0, tsum / jnp.where(hits > 0, root, 1.0), 0.0)
    taps_in.wait()
    fill_band(taps, band)
    shift = jnp.concatenate([bias[...]] * 4, axis=1)
    waited = 0
    for cx in range(2):
        while waited < 2 * cx + 4:
            copies[waited].wait()
            waited += 1
        for cy in range(2):
            lhs = jnp.concatenate(
                [
                    slab[2 * cx + dx : 2 * cx + dx + 2, 2 * cy + dy : 2 * cy + dy + 2].reshape(
                        4 * NP, EDGE * C
                    )
                    for dx in range(3)
                    for dy in range(3)
                ],
                axis=1,
            )
            act = jnp.tanh(dot(lhs, band[...]) + shift).reshape(4, NP, 4 * C)
            pooled = (act[0] + act[1]) + (act[2] + act[3])
            cell = (pooled[:, : 2 * C] + pooled[:, 2 * C :]) * 0.125
            feats[:, (2 * cx + cy) * 2 * C : (2 * cx + cy + 1) * 2 * C] = cell

    rows = feats[:HIT, :]
    peak = jnp.max(jnp.abs(rows), axis=1, keepdims=True)
    unit = jnp.where(peak > 0, TOP / jnp.where(peak > 0, peak, 1.0), 0.0)
    pay[...] = jnp.round(rows * unit).astype(jnp.int32).astype(jnp.int16)
    lane = iota((HIT, 128), 1)
    sides = jnp.where(lane == 0, scaled, jnp.where(lane == 1, peak * (root * (1.0 / TOP)), 0.0))
    aux[...] = jnp.concatenate([sides.T[:8, :], jnp.zeros((8, 128 - HIT), F32)], axis=1)
    pick = (iota((NP, NQ), 0) == qids[...]).astype(F32).astype(BF16)
    qrows[...] = dot(pick, feats[...].astype(BF16), 0, 0).astype(BF16)


def spread(x, shape=(8, 128)):
    return jnp.broadcast_to(x, shape)


def inverse_factor(gram):
    n = gram.shape[0]
    eye = jnp.where(iota((n, n), 0) == iota((n, n), 1), 1.0, 0.0)
    parts = [gram, eye] if n == 64 else [gram, eye, jnp.zeros((n, 128 - 2 * n), F32)]
    wide = jnp.concatenate(parts, axis=1)
    sub = iota((8, 128), 0)
    count = n // 8
    rows = [wide[8 * b : 8 * b + 8] for b in range(count)]
    done = []
    for b in range(count):
        cols = [
            [spread(rows[t][:, 8 * b + c : 8 * b + c + 1]) for c in range(8)] for t in range(b, count)
        ]
        for j in range(8):
            heads = [spread(cols[0][c][j : j + 1, :]) for c in range(j, 8)]
            inv = 1.0 / heads[0]
            row = spread(rows[b][j : j + 1, :]) * inv
            heads = [h * inv for h in heads]
            for t in range(count - b):
                below = jnp.where(sub > j, cols[0][j], 0.0) if t == 0 else cols[t][j]
                rows[b + t] = rows[b + t] - below * row
                for c in range(j + 1, 8):
                    cols[t][c] = cols[t][c] - below * heads[c - j]
        diag = cols[0][0]
        for j in range(1, 8):
            diag = jnp.where(sub == j, cols[0][j], diag)
        done.append(rows[b] * lax.rsqrt(diag))
    return jnp.concatenate(done, axis=0)[:, n : 2 * n]


def eliminate(codes, sides, at, first, t_hi, t_lo, tt_hi, tt_lo, tt_row):
    n = codes.shape[0]
    column = jnp.concatenate([side.T[:HIT] for side in sides], axis=0)
    a_hi, a_lo = split2(codes.astype(jnp.int32).astype(F32) * column[:, 1:2])
    rest = jnp.concatenate(
        [
            a_hi.astype(F32) + a_lo.astype(F32),
            jnp.where(iota((n, 128), 1) == 0, column[:, 0:1], 0.0),
        ],
        axis=1,
    )
    both = jnp.concatenate([a_hi, a_lo], axis=0)
    gg = dot(both, both, 1, 1)
    gram = gg[:n, :n] + (gg[:n, n:] + gg[n:, :n])
    gram = gram + jnp.where(iota((n, n), 0) == iota((n, n), 1), 8.0, 0.0)
    if not first:
        part = dot(both, tt_hi[:F, :])
        low = part[:n] + (part[n:] + dot(a_hi, tt_lo[:F, :]))
        gram = gram - dot(low, low, 1, 1, HIGHEST)
        l_hi, l_lo = split2(low)
        part = dot(jnp.concatenate([l_hi, l_lo], axis=0), t_hi[...])
        rest = rest - (part[:n] + (part[n:] + dot(l_hi, t_lo[...])))
    rows = dot(inverse_factor(gram), rest, 1, 0, HIGHEST)
    r_hi, r_lo = split2(rows)
    t_hi[at : at + n, :] = r_hi
    t_lo[at : at + n, :] = r_lo
    cols = rows.T
    c_hi, c_lo = split2(cols)
    tt_hi[:, at : at + n] = c_hi
    tt_lo[:, at : at + n] = c_lo
    tt_row[:, at : at + n] = cols[F : F + 8, :]


def evaluate(queries, tt_hi, tt_lo, tt_row):
    y = tt_row[0:1, :]
    var, mean = [], []
    for i in range(2):
        x = queries[8 * i : 8 * i + 8].reshape(8 * NQ, F)
        t = dot(x, tt_hi[:F, :]) + dot(x, tt_lo[:F, :])
        xf = x.astype(F32)
        t0, t1 = t[:, :128], t[:, 128:]
        sq = xf * xf
        sv = (sq[:, :128] + sq[:, 128:256]) + (sq[:, 256:384] + sq[:, 384:]) - (t0 * t0 + t1 * t1)
        sm = t0 * y[:, :128] + t1 * y[:, 128:]
        for part, lines in ((sv, var), (sm, mean)):
            for b in range(4):
                lines.append(jnp.sum(part[128 * b : 128 * b + 128].T, axis=0, keepdims=True))
    return jnp.concatenate(var, axis=0), jnp.concatenate(mean, axis=0)


def group_kernel(
    n_mem, count, vox, weight, bias, ids, targets, qids, out,
    slab, taps, band, feats, blocks, sides, queries, t_hi, t_lo, tt_hi, tt_lo, tt_row,
    sem, wsem, bsend, brecv, ssend, srecv, psend, precv, lsend, lrecv, csend, crecv,
):
    g, m = lax.axis_index("grp"), lax.axis_index("mem")
    core, plane = lax.rem(g, 2), lax.div(g, 2)
    px, py = lax.rem(plane, 4), lax.div(plane, 4)
    zs = [lax.rem(m + n_mem + d, n_mem) for d in (1, -1, 2, -2, 3, -3, 4)]
    xs = [(py * 4 + lax.rem(px + s, 4)) * 2 + core for s in (1, 2, 3)]
    ys = [(lax.rem(py + s, 4) * 4 + px) * 2 + core for s in (1, 2, 3)]
    other = plane * 2 + (1 - core)

    barrier = pltpu.get_barrier_semaphore()
    for peer in [(g, z) for z in zs] + [(h, m) for h in xs + ys + [other]]:
        pl.semaphore_signal(barrier, inc=1, device_id=peer, device_id_type=MESH)

    factor = (t_hi, t_lo, tt_hi, tt_lo, tt_row)
    for ref in factor:
        ref[...] = jnp.zeros_like(ref)
    pay, aux, qrows = blocks.at[0], sides.at[0], queries.at[core, py, px]
    features(
        count, vox, weight, bias, ids, targets, qids, pay, aux, qrows, slab, taps, band, feats, sem, wsem
    )
    pl.semaphore_wait(barrier, 14)

    def remote(src, dst, send, recv, peer):
        return pltpu.make_async_remote_copy(
            src_ref=src, dst_ref=dst, send_sem=send, recv_sem=recv, device_id=peer, device_id_type=MESH
        )

    hops = []
    for i, z in enumerate(zs):
        hops.append(
            (
                remote(pay, blocks.at[i + 1], bsend.at[i], brecv.at[i], (g, z)),
                remote(aux, sides.at[i + 1], ssend.at[i], srecv.at[i], (g, z)),
            )
        )
    for codes, side in hops:
        side.start()
        codes.start()

    half = NQ // 2
    top, bottom = pl.ds(0, half), pl.ds(half, half)
    near = [
        remote(qrows.at[top], queries.at[core, py, px, top], psend.at[i], precv.at[i], (xs[i], m))
        for i in range(3)
    ] + [
        remote(
            qrows.at[bottom], queries.at[core, py, px, bottom], psend.at[3 + i], precv.at[3 + i], (ys[i], m)
        )
        for i in range(3)
    ]
    row, column = queries.at[core, py, :, top], queries.at[core, :, px, bottom]
    far = [remote(row, row, lsend.at[i], lrecv.at[i], (ys[i], m)) for i in range(3)] + [
        remote(column, column, lsend.at[3 + i], lrecv.at[3 + i], (xs[i], m)) for i in range(3)
    ]
    pieces = []
    for i, shift in enumerate((0, 1, 2, 3)):
        wy, wx = lax.rem(py + 4 - shift, 4), lax.rem(px + 4 - shift, 4)
        for j, piece in enumerate((queries.at[core, wy, :, top], queries.at[core, :, wx, bottom])):
            pieces.append(remote(piece, piece, csend.at[2 * i + j], crecv.at[2 * i + j], (other, m)))
    for copy in near:
        copy.start()

    def step(slots, at):
        for slot in slots:
            if slot > 0:
                hops[slot - 1][0].wait_recv()
                hops[slot - 1][1].wait_recv()
        lo, hi = slots[0], slots[-1] + 1
        eliminate(
            blocks[lo:hi].reshape((hi - lo) * HIT, F), [sides[i] for i in slots], at, lo == 0, *factor
        )

    step((0,), 192)
    for copy in near:
        copy.wait_recv()
    for i in (0, 3, 2, 5, 1, 4):
        far[i].start()
    for copy in pieces[:2]:
        copy.start()
    step((1, 2), 0)
    step((3, 4), 64)
    for i in (0, 2):
        for j in range(2):
            far[3 * j + i].wait_recv()
            pieces[2 * (i + 1) + j].start()
    step((5, 6), 128)
    for j in range(2):
        far[3 * j + 1].wait_recv()
        pieces[4 + j].start()
    step((7,), 224)

    def half_lines(which):
        return evaluate(queries.at[which].reshape(16, NQ, F), tt_hi, tt_lo, tt_row)

    near_half = half_lines(core)
    for copy in pieces:
        copy.wait_recv()
    far_half = half_lines(1 - core)
    for i in range(2):
        even = jnp.where(core == 0, near_half[i], far_half[i])
        odd = jnp.where(core == 0, far_half[i], near_half[i])
        for side in range(2):
            lanes = slice(NQ * side, NQ * (side + 1))
            out[i, pl.ds(side, 8, stride=2), :] = jnp.concatenate([even[:, lanes], odd[:, lanes]], axis=1)

    for codes, side in hops:
        codes.wait_send()
        side.wait_send()
    for copy in near + far + pieces:
        copy.wait_send()


def group_posterior(n_mem, count, vox, weight, bias, ids, targets, qids):
    vmem, hbm = pl.BlockSpec(memory_space=pltpu.VMEM), pl.BlockSpec(memory_space=pl.ANY)
    dma = pltpu.SemaphoreType.DMA
    return pl.pallas_call(
        functools.partial(group_kernel, n_mem),
        out_shape=jax.ShapeDtypeStruct((2, 16, 128), F32),
        in_specs=[pl.BlockSpec(memory_space=pltpu.SMEM), hbm, hbm, vmem, vmem, vmem, vmem],
        out_specs=vmem,
        scratch_shapes=[
            pltpu.VMEM((EDGE, EDGE, NP, EDGE * C), BF16),
            pltpu.VMEM((3, 3, 3, C, C), BF16),
            pltpu.VMEM((9 * EDGE * C, 4 * C), BF16),
            pltpu.VMEM((NP, F), F32),
            pltpu.VMEM((n_mem, HIT, F), jnp.int16),
            pltpu.VMEM((n_mem, 8, 128), F32),
            pltpu.VMEM((2, 4, 4, NQ, F), BF16),
            pltpu.VMEM((256, FU), BF16),
            pltpu.VMEM((256, FU), BF16),
            pltpu.VMEM((FU, 256), BF16),
            pltpu.VMEM((FU, 256), BF16),
            pltpu.VMEM((8, 256), F32),
            dma((EDGE,)), dma((1,)), dma((7,)), dma((7,)), dma((7,)), dma((7,)),
            dma((6,)), dma((6,)), dma((6,)), dma((6,)), dma((8,)), dma((8,)),
        ],
        compiler_params=pltpu.CompilerParams(
            collective_id=0, has_side_effects=True, vmem_limit_bytes=63 << 20
        ),
        name="group_posterior",
    )(count, vox, weight, bias, ids, targets, qids)


def on_device(n_mem, voxels, conv_weight, conv_bias, row_counts, sample_patch, targets, query_patch):
    out = group_posterior(
        n_mem,
        row_counts,
        voxels.transpose(1, 2, 0, 3),
        conv_weight,
        conv_bias.reshape(1, C),
        sample_patch.reshape(1, -1),
        targets.reshape(1, -1),
        query_patch.reshape(1, -1),
    )
    return out[0].reshape(1, 1, -1), out[1].reshape(1, 1, -1)


def solution(mesh):
    rows = ("grp", "mem")
    in_specs = (P(rows, None, None, None), P(), P(), P(rows), P(rows), P(rows), P(rows))
    out_specs = (P("grp", "mem", None), P("grp", "mem", None))
    return jax.shard_map(
        functools.partial(on_device, mesh.shape["mem"]),
        mesh=mesh,
        in_specs=in_specs,
        out_specs=out_specs,
        check_vma=False,
    )
```

```python
import functools

import jax
import jax.numpy as jnp
from jax import lax
from jax.experimental import pallas as pl
from jax.experimental.pallas import tpu as pltpu
from jax.sharding import PartitionSpec as P

C = 64
EDGE = 6
NP = 128
HIT = 32
F = 512
NQ = 64
FU = F + 128
TOP = 32767.0
MESH = pl.DeviceIdType.MESH
F32 = jnp.float32
BF16 = jnp.bfloat16
HIGHEST = lax.Precision.HIGHEST


def iota(shape, dim):
    return lax.broadcasted_iota(jnp.int32, shape, dim)


def split2(x):
    hi = x.astype(BF16)
    return hi, (x - hi.astype(F32)).astype(BF16)


def dot(a, b, ca=1, cb=0, precision=None):
    return lax.dot_general(
        a, b, (((ca,), (cb,)), ((), ())), precision=precision, preferred_element_type=F32
    )


def fill_band(weight, band):
    zero = jnp.zeros((C, C), BF16)
    for dx in range(3):
        for dy in range(3):
            taps = [weight[dx, dy, dz] for dz in range(3)]
            at = lambda d: taps[d] if 0 <= d <= 2 else zero
            for zi in range(EDGE):
                row = (dx * 3 + dy) * EDGE * C + zi * C
                band[row : row + C, : 2 * C] = jnp.concatenate([at(zi), at(zi - 2)], axis=1)
                band[row : row + C, 2 * C :] = jnp.concatenate([at(zi - 1), at(zi - 3)], axis=1)


def patch_features(slab, band, shift, part, feats):
    own = slice(HIT * part, HIT * (part + 1))
    lhs = jnp.concatenate(
        [
            slab[dx : dx + 4, dy : dy + 4, own].reshape(16 * HIT, EDGE * C)
            for dx in range(3)
            for dy in range(3)
        ],
        axis=1,
    )
    act = jnp.tanh(dot(lhs, band[...]) + shift).reshape(2, 2, 2, 2, HIT, 4 * C)
    for cx in range(2):
        for cy in range(2):
            cell = (act[cx, 0, cy, 0] + act[cx, 0, cy, 1]) + (act[cx, 1, cy, 0] + act[cx, 1, cy, 1])
            at = (2 * cx + cy) * 2 * C
            feats[own, at : at + 2 * C] = (cell[:, : 2 * C] + cell[:, 2 * C :]) * 0.125


def hit_sums(count, ids, targets):
    live = iota((HIT, ids.shape[1]), 1) < count[0]
    mine = jnp.logical_and(ids[...] == iota((HIT, ids.shape[1]), 0), live)
    hits = jnp.sum(jnp.where(mine, 1.0, 0.0), axis=1, keepdims=True)
    tsum = jnp.sum(jnp.where(mine, targets[...], 0.0), axis=1, keepdims=True)
    root = jnp.sqrt(hits)
    return root, jnp.where(hits > 0, tsum / jnp.where(hits > 0, root, 1.0), 0.0)


def code_rows(rows, root, scaled, pay, aux):
    peak = jnp.max(jnp.abs(rows), axis=1, keepdims=True)
    unit = jnp.where(peak > 0, TOP / jnp.where(peak > 0, peak, 1.0), 0.0)
    pay[...] = jnp.round(rows * unit).astype(jnp.int32).astype(jnp.int16)
    lane = iota((HIT, 128), 1)
    sides = jnp.where(lane == 0, scaled, jnp.where(lane == 1, peak * (root * (1.0 / TOP)), 0.0))
    aux[...] = jnp.concatenate([sides.T[:8, :], jnp.zeros((8, 128 - HIT), F32)], axis=1)


def spread(x, shape=(8, 128)):
    return jnp.broadcast_to(x, shape)


def inverse_factor(gram):
    n = gram.shape[0]
    eye = jnp.where(iota((n, n), 0) == iota((n, n), 1), 1.0, 0.0)
    parts = [gram, eye] if n == 64 else [gram, eye, jnp.zeros((n, 128 - 2 * n), F32)]
    wide = jnp.concatenate(parts, axis=1)
    sub = iota((8, 128), 0)
    count = n // 8
    rows = [wide[8 * b : 8 * b + 8] for b in range(count)]

    def columns(t, b):
        return [spread(rows[t][:, 8 * b + c : 8 * b + c + 1]) for c in range(8)]

    done = []
    diagonal = columns(0, 0)
    for b in range(count):
        cols = {t: columns(t, b) for t in range(b + 1, count)}
        cols[b] = diagonal
        ahead = b + 1 < count
        if ahead:
            coming, taken = columns(b + 1, b + 1), [None] * 8
        for j in range(8):
            heads = [spread(cols[b][c][j : j + 1, :]) for c in range(j, 8)]
            inv = 1.0 / heads[0]
            times = {
                t: (jnp.where(sub > j, cols[t][j], 0.0) if t == b else cols[t][j]) * inv
                for t in range(b, count)
            }
            row = spread(rows[b][j : j + 1, :])
            for t in range(b, count):
                for c in range(j + 1, 8):
                    cols[t][c] = cols[t][c] - times[t] * heads[c - j]
            for t in range(b, count):
                rows[t] = rows[t] - times[t] * row
            if ahead:
                for c in range(8):
                    term = times[b + 1] * spread(cols[b + 1][j][c : c + 1, :])
                    taken[c] = term if taken[c] is None else taken[c] + term
        pivots = cols[b][0]
        for j in range(1, 8):
            pivots = jnp.where(sub == j, cols[b][j], pivots)
        done.append(rows[b] * lax.rsqrt(pivots))
        if ahead:
            diagonal = [coming[c] - taken[c] for c in range(8)]
    return jnp.concatenate(done, axis=0)[:, n : 2 * n]


def eliminate(codes, sides, at, first, t_hi, t_lo, tt_hi, tt_lo, tt_row):
    n = codes.shape[0]
    column = jnp.concatenate([side.T[:HIT] for side in sides], axis=0)
    a_hi, a_lo = split2(codes.astype(jnp.int32).astype(F32) * column[:, 1:2])
    rest = jnp.concatenate(
        [
            a_hi.astype(F32) + a_lo.astype(F32),
            jnp.where(iota((n, 128), 1) == 0, column[:, 0:1], 0.0),
        ],
        axis=1,
    )
    both = jnp.concatenate([a_hi, a_lo], axis=0)
    gg = dot(both, both, 1, 1)
    gram = gg[:n, :n] + (gg[:n, n:] + gg[n:, :n])
    gram = gram + jnp.where(iota((n, n), 0) == iota((n, n), 1), 8.0, 0.0)
    if not first:
        part = dot(both, tt_hi[:F, :])
        low = part[:n] + (part[n:] + dot(a_hi, tt_lo[:F, :]))
        gram = gram - dot(low, low, 1, 1, HIGHEST)
        l_hi, l_lo = split2(low)
        part = dot(jnp.concatenate([l_hi, l_lo], axis=0), t_hi[...])
        rest = rest - (part[:n] + (part[n:] + dot(l_hi, t_lo[...])))
    rows = dot(inverse_factor(gram), rest, 1, 0, HIGHEST)
    r_hi, r_lo = split2(rows)
    t_hi[at : at + n, :] = r_hi
    t_lo[at : at + n, :] = r_lo
    cols = rows.T
    c_hi, c_lo = split2(cols)
    tt_hi[:, at : at + n] = c_hi
    tt_lo[:, at : at + n] = c_lo
    tt_row[:, at : at + n] = cols[F : F + 8, :]


def evaluate(queries, tt_hi, tt_lo, tt_row):
    y = tt_row[0:1, :]
    var, mean = [], []
    for i in range(2):
        x = queries[8 * i : 8 * i + 8].reshape(8 * NQ, F)
        t = dot(x, tt_hi[:F, :]) + dot(x, tt_lo[:F, :])
        xf = x.astype(F32)
        t0, t1 = t[:, :128], t[:, 128:]
        sq = xf * xf
        sv = (sq[:, :128] + sq[:, 128:256]) + (sq[:, 256:384] + sq[:, 384:]) - (t0 * t0 + t1 * t1)
        sm = t0 * y[:, :128] + t1 * y[:, 128:]
        for part, lines in ((sv, var), (sm, mean)):
            for b in range(4):
                lines.append(jnp.sum(part[128 * b : 128 * b + 128].T, axis=0, keepdims=True))
    return jnp.concatenate(var, axis=0), jnp.concatenate(mean, axis=0)


def group_kernel(
    n_mem, count, vox, weight, bias_in, ids_in, targets_in, qids_in, out,
    bias, ids, targets, qids, slab, taps, band, feats, blocks, sides, queries, t_hi, t_lo, tt_hi, tt_lo, tt_row,
    sem, wsem, bsend, brecv, ssend, srecv, psend, precv, lsend, lrecv, csend, crecv,
):
    g, m = lax.axis_index("grp"), lax.axis_index("mem")
    core, plane = lax.rem(g, 2), lax.div(g, 2)
    px, py = lax.rem(plane, 4), lax.div(plane, 4)
    zs = [lax.rem(m + n_mem + d, n_mem) for d in (1, -1, 2, -2, 3, -3, 4)]
    xs = [(py * 4 + lax.rem(px + s, 4)) * 2 + core for s in (1, 2, 3)]
    ys = [(lax.rem(py + s, 4) * 4 + px) * 2 + core for s in (1, 2, 3)]
    other = plane * 2 + (1 - core)

    barrier = pltpu.get_barrier_semaphore()
    for peer in [(g, z) for z in zs] + [(h, m) for h in xs + ys + [other]]:
        pl.semaphore_signal(barrier, inc=1, device_id=peer, device_id_type=MESH)

    taps_in = pltpu.make_async_copy(weight, taps, wsem.at[0])
    small = [
        pltpu.make_async_copy(src, dst, wsem.at[i + 1])
        for i, (src, dst) in enumerate(
            ((bias_in, bias), (ids_in, ids), (targets_in, targets), (qids_in, qids))
        )
    ]
    for copy in [taps_in] + small:
        copy.start()
    parts = []
    for p in range(NP // HIT):
        own = pl.ds(HIT * p, HIT)
        parts.append(pltpu.make_async_copy(vox.at[:, :, own], slab.at[:, :, own], sem.at[p]))
        parts[p].start()

    factor = (t_hi, t_lo, tt_hi, tt_lo, tt_row)
    for ref in factor:
        ref[...] = jnp.zeros_like(ref)
    for copy in small:
        copy.wait()
    root, scaled = hit_sums(count, ids, targets)
    shift = jnp.concatenate([bias[...]] * 4, axis=1)
    taps_in.wait()
    fill_band(taps, band)
    pay, aux, qrows = blocks.at[0], sides.at[0], queries.at[core, py, px]

    parts[0].wait()
    patch_features(slab, band, shift, 0, feats)
    code_rows(feats[:HIT, :], root, scaled, pay, aux)
    pl.semaphore_wait(barrier, 14)

    def remote(src, dst, send, recv, peer):
        return pltpu.make_async_remote_copy(
            src_ref=src, dst_ref=dst, send_sem=send, recv_sem=recv, device_id=peer, device_id_type=MESH
        )

    hops = []
    for i, z in enumerate(zs):
        hops.append(
            (
                remote(pay, blocks.at[i + 1], bsend.at[i], brecv.at[i], (g, z)),
                remote(aux, sides.at[i + 1], ssend.at[i], srecv.at[i], (g, z)),
            )
        )
    for codes, side in hops:
        side.start()
        codes.start()

    for p in range(1, NP // HIT):
        parts[p].wait()
        patch_features(slab, band, shift, p, feats)
    pick = (iota((NP, NQ), 0) == qids[...]).astype(F32).astype(BF16)
    qrows[...] = dot(pick, feats[...].astype(BF16), 0, 0).astype(BF16)

    half = NQ // 2
    top, bottom = pl.ds(0, half), pl.ds(half, half)
    near = [
        remote(qrows.at[top], queries.at[core, py, px, top], psend.at[i], precv.at[i], (xs[i], m))
        for i in range(3)
    ] + [
        remote(
            qrows.at[bottom], queries.at[core, py, px, bottom], psend.at[3 + i], precv.at[3 + i], (ys[i], m)
        )
        for i in range(3)
    ]
    row, column = queries.at[core, py, :, top], queries.at[core, :, px, bottom]
    far = [remote(row, row, lsend.at[i], lrecv.at[i], (ys[i], m)) for i in range(3)] + [
        remote(column, column, lsend.at[3 + i], lrecv.at[3 + i], (xs[i], m)) for i in range(3)
    ]
    pieces = []
    for i, shift in enumerate((0, 1, 2, 3)):
        wy, wx = lax.rem(py + 4 - shift, 4), lax.rem(px + 4 - shift, 4)
        for j, piece in enumerate((queries.at[core, wy, :, top], queries.at[core, :, wx, bottom])):
            pieces.append(remote(piece, piece, csend.at[2 * i + j], crecv.at[2 * i + j], (other, m)))
    for copy in near:
        copy.start()

    def step(slots, at):
        for slot in slots:
            if slot > 0:
                hops[slot - 1][0].wait_recv()
                hops[slot - 1][1].wait_recv()
        lo, hi = slots[0], slots[-1] + 1
        eliminate(
            blocks[lo:hi].reshape((hi - lo) * HIT, F), [sides[i] for i in slots], at, lo == 0, *factor
        )

    step((0,), 192)
    step((1, 2), 0)
    for copy in near:
        copy.wait_recv()
    for i in (0, 3, 2, 5, 1, 4):
        far[i].start()
    for copy in pieces[:2]:
        copy.start()
    step((3, 4), 64)
    step((5, 6), 128)
    for i in (0, 2):
        for j in range(2):
            far[3 * j + i].wait_recv()
            pieces[2 * (i + 1) + j].start()
    step((7,), 224)
    for j in range(2):
        far[3 * j + 1].wait_recv()
        pieces[4 + j].start()

    def half_lines(which):
        return evaluate(queries.at[which].reshape(16, NQ, F), tt_hi, tt_lo, tt_row)

    near_half = half_lines(core)
    for copy in pieces:
        copy.wait_recv()
    far_half = half_lines(1 - core)
    for i in range(2):
        even = jnp.where(core == 0, near_half[i], far_half[i])
        odd = jnp.where(core == 0, far_half[i], near_half[i])
        for side in range(2):
            lanes = slice(NQ * side, NQ * (side + 1))
            out[i, pl.ds(side, 8, stride=2), :] = jnp.concatenate([even[:, lanes], odd[:, lanes]], axis=1)

    for codes, side in hops:
        codes.wait_send()
        side.wait_send()
    for copy in near + far + pieces:
        copy.wait_send()


def group_posterior(n_mem, count, vox, weight, bias, ids, targets, qids):
    vmem, hbm = pl.BlockSpec(memory_space=pltpu.VMEM), pl.BlockSpec(memory_space=pltpu.HBM)
    dma = pltpu.SemaphoreType.DMA
    return pl.pallas_call(
        functools.partial(group_kernel, n_mem),
        out_shape=jax.ShapeDtypeStruct((2, 16, 128), F32),
        in_specs=[pl.BlockSpec(memory_space=pltpu.SMEM), hbm, hbm, hbm, hbm, hbm, hbm],
        out_specs=vmem,
        scratch_shapes=[
            pltpu.VMEM((1, C), F32),
            pltpu.VMEM(ids.shape, jnp.int32),
            pltpu.VMEM(ids.shape, F32),
            pltpu.VMEM((1, NQ), jnp.int32),
            pltpu.VMEM((EDGE, EDGE, NP, EDGE * C), BF16),
            pltpu.VMEM((3, 3, 3, C, C), BF16),
            pltpu.VMEM((9 * EDGE * C, 4 * C), BF16),
            pltpu.VMEM((NP, F), F32),
            pltpu.VMEM((n_mem, HIT, F), jnp.int16),
            pltpu.VMEM((n_mem, 8, 128), F32),
            pltpu.VMEM((2, 4, 4, NQ, F), BF16),
            pltpu.VMEM((256, FU), BF16),
            pltpu.VMEM((256, FU), BF16),
            pltpu.VMEM((FU, 256), BF16),
            pltpu.VMEM((FU, 256), BF16),
            pltpu.VMEM((8, 256), F32),
            dma((NP // HIT,)), dma((5,)), dma((7,)), dma((7,)), dma((7,)), dma((7,)),
            dma((6,)), dma((6,)), dma((6,)), dma((6,)), dma((8,)), dma((8,)),
        ],
        compiler_params=pltpu.CompilerParams(
            collective_id=0, has_side_effects=True, vmem_limit_bytes=61 << 20
        ),
        name="group_posterior",
    )(count, vox, weight, bias, ids, targets, qids)


def on_device(n_mem, voxels, conv_weight, conv_bias, row_counts, sample_patch, targets, query_patch):
    out = group_posterior(
        n_mem,
        row_counts,
        voxels.transpose(1, 2, 0, 3),
        conv_weight,
        conv_bias.reshape(1, C),
        sample_patch.reshape(1, -1),
        targets.reshape(1, -1),
        query_patch.reshape(1, -1),
    )
    return out[0].reshape(1, 1, -1), out[1].reshape(1, 1, -1)


def solution(mesh):
    rows = ("grp", "mem")
    in_specs = (P(rows, None, None, None), P(), P(), P(rows), P(rows), P(rows), P(rows))
    out_specs = (P("grp", "mem", None), P("grp", "mem", None))
    return jax.shard_map(
        functools.partial(on_device, mesh.shape["mem"]),
        mesh=mesh,
        in_specs=in_specs,
        out_specs=out_specs,
        check_vma=False,
    )
```

```python
import functools

import jax
import jax.numpy as jnp
from jax import lax
from jax.experimental import pallas as pl
from jax.experimental.pallas import tpu as pltpu
from jax.sharding import PartitionSpec as P

C = 64
EDGE = 6
NP = 128
HIT = 32
F = 512
NQ = 64
FU = F + 128
TOP = 32767.0
MESH = pl.DeviceIdType.MESH
F32 = jnp.float32
BF16 = jnp.bfloat16
HIGHEST = lax.Precision.HIGHEST


def iota(shape, dim):
    return lax.broadcasted_iota(jnp.int32, shape, dim)


def split2(x):
    hi = x.astype(BF16)
    return hi, (x - hi.astype(F32)).astype(BF16)


def dot(a, b, ca=1, cb=0, precision=None):
    return lax.dot_general(
        a, b, (((ca,), (cb,)), ((), ())), precision=precision, preferred_element_type=F32
    )


def fill_band(weight, band):
    zero = jnp.zeros((C, C), BF16)
    for dx in range(3):
        for dy in range(3):
            taps = [weight[dx, dy, dz] for dz in range(3)]
            at = lambda d: taps[d] if 0 <= d <= 2 else zero
            for zi in range(EDGE):
                row = (dx * 3 + dy) * EDGE * C + zi * C
                band[row : row + C, : 2 * C] = jnp.concatenate([at(zi), at(zi - 2)], axis=1)
                band[row : row + C, 2 * C :] = jnp.concatenate([at(zi - 1), at(zi - 3)], axis=1)


def features(
    count, vox, weight, bias, ids, targets, qids, pay, aux, qrows, slab, taps, band, feats, sem, wsem
):
    copies = [pltpu.make_async_copy(vox.at[x], slab.at[x], sem.at[x]) for x in range(EDGE)]
    taps_in = pltpu.make_async_copy(weight, taps, wsem.at[0])
    taps_in.start()
    for copy in copies:
        copy.start()

    live = iota((HIT, ids.shape[1]), 1) < count[0]
    mine = jnp.logical_and(ids[...] == iota((HIT, ids.shape[1]), 0), live)
    hits = jnp.sum(jnp.where(mine, 1.0, 0.0), axis=1, keepdims=True)
    tsum = jnp.sum(jnp.where(mine, targets[...], 0.0), axis=1, keepdims=True)
    root = jnp.sqrt(hits)
    scaled = jnp.where(hits > 0, tsum / jnp.where(hits > 0, root, 1.0), 0.0)
    taps_in.wait()
    fill_band(taps, band)
    shift = jnp.concatenate([bias[...]] * 4, axis=1)
    waited = 0
    for cx in range(2):
        while waited < 2 * cx + 4:
            copies[waited].wait()
            waited += 1
        for cy in range(2):
            lhs = jnp.concatenate(
                [
                    slab[2 * cx + dx : 2 * cx + dx + 2, 2 * cy + dy : 2 * cy + dy + 2].reshape(
                        4 * NP, EDGE * C
                    )
                    for dx in range(3)
                    for dy in range(3)
                ],
                axis=1,
            )
            act = jnp.tanh(dot(lhs, band[...]) + shift).reshape(4, NP, 4 * C)
            pooled = (act[0] + act[1]) + (act[2] + act[3])
            cell = (pooled[:, : 2 * C] + pooled[:, 2 * C :]) * 0.125
            feats[:, (2 * cx + cy) * 2 * C : (2 * cx + cy + 1) * 2 * C] = cell

    rows = feats[:HIT, :]
    peak = jnp.max(jnp.abs(rows), axis=1, keepdims=True)
    unit = jnp.where(peak > 0, TOP / jnp.where(peak > 0, peak, 1.0), 0.0)
    pay[...] = jnp.round(rows * unit).astype(jnp.int32).astype(jnp.int16)
    lane = iota((HIT, 128), 1)
    sides = jnp.where(lane == 0, scaled, jnp.where(lane == 1, peak * (root * (1.0 / TOP)), 0.0))
    aux[...] = jnp.concatenate([sides.T[:8, :], jnp.zeros((8, 128 - HIT), F32)], axis=1)
    pick = (iota((NP, NQ), 0) == qids[...]).astype(F32).astype(BF16)
    qrows[...] = dot(pick, feats[...].astype(BF16), 0, 0).astype(BF16)


def spread(x, shape=(8, 128)):
    return jnp.broadcast_to(x, shape)


def inverse_factor(gram):
    n = gram.shape[0]
    eye = jnp.where(iota((n, n), 0) == iota((n, n), 1), 1.0, 0.0)
    parts = [gram, eye] if n == 64 else [gram, eye, jnp.zeros((n, 128 - 2 * n), F32)]
    wide = jnp.concatenate(parts, axis=1)
    sub = iota((8, 128), 0)
    count = n // 8
    rows = [wide[8 * b : 8 * b + 8] for b in range(count)]

    def columns(t, b):
        return [spread(rows[t][:, 8 * b + c : 8 * b + c + 1]) for c in range(8)]

    done = []
    diagonal = columns(0, 0)
    for b in range(count):
        cols = {t: columns(t, b) for t in range(b + 1, count)}
        cols[b] = diagonal
        ahead = b + 1 < count
        if ahead:
            coming, taken = columns(b + 1, b + 1), [None] * 8
        for j in range(8):
            heads = [spread(cols[b][c][j : j + 1, :]) for c in range(j, 8)]
            inv = 1.0 / heads[0]
            times = {
                t: (jnp.where(sub > j, cols[t][j], 0.0) if t == b else cols[t][j]) * inv
                for t in range(b, count)
            }
            row = spread(rows[b][j : j + 1, :])
            for t in range(b, count):
                for c in range(j + 1, 8):
                    cols[t][c] = cols[t][c] - times[t] * heads[c - j]
            for t in range(b, count):
                rows[t] = rows[t] - times[t] * row
            if ahead:
                for c in range(8):
                    term = times[b + 1] * spread(cols[b + 1][j][c : c + 1, :])
                    taken[c] = term if taken[c] is None else taken[c] + term
        pivots = cols[b][0]
        for j in range(1, 8):
            pivots = jnp.where(sub == j, cols[b][j], pivots)
        done.append(rows[b] * lax.rsqrt(pivots))
        if ahead:
            diagonal = [coming[c] - taken[c] for c in range(8)]
    return jnp.concatenate(done, axis=0)[:, n : 2 * n]


def eliminate(codes, sides, at, first, t_hi, t_lo, tt_hi, tt_lo, tt_row):
    n = codes.shape[0]
    column = jnp.concatenate([side.T[:HIT] for side in sides], axis=0)
    a_hi, a_lo = split2(codes.astype(jnp.int32).astype(F32) * column[:, 1:2])
    rest = jnp.concatenate(
        [
            a_hi.astype(F32) + a_lo.astype(F32),
            jnp.where(iota((n, 128), 1) == 0, column[:, 0:1], 0.0),
        ],
        axis=1,
    )
    both = jnp.concatenate([a_hi, a_lo], axis=0)
    gg = dot(both, both, 1, 1)
    gram = gg[:n, :n] + (gg[:n, n:] + gg[n:, :n])
    gram = gram + jnp.where(iota((n, n), 0) == iota((n, n), 1), 8.0, 0.0)
    if not first:
        part = dot(both, tt_hi[:F, :])
        low = part[:n] + (part[n:] + dot(a_hi, tt_lo[:F, :]))
        gram = gram - dot(low, low, 1, 1, HIGHEST)
        l_hi, l_lo = split2(low)
        part = dot(jnp.concatenate([l_hi, l_lo], axis=0), t_hi[...])
        rest = rest - (part[:n] + (part[n:] + dot(l_hi, t_lo[...])))
    rows = dot(inverse_factor(gram), rest, 1, 0, HIGHEST)
    r_hi, r_lo = split2(rows)
    t_hi[at : at + n, :] = r_hi
    t_lo[at : at + n, :] = r_lo
    cols = rows.T
    c_hi, c_lo = split2(cols)
    tt_hi[:, at : at + n] = c_hi
    tt_lo[:, at : at + n] = c_lo
    tt_row[:, at : at + n] = cols[F : F + 8, :]


def evaluate(queries, tt_hi, tt_lo, tt_row):
    y = tt_row[0:1, :]
    var, mean = [], []
    for i in range(2):
        x = queries[8 * i : 8 * i + 8].reshape(8 * NQ, F)
        t = dot(x, tt_hi[:F, :]) + dot(x, tt_lo[:F, :])
        xf = x.astype(F32)
        t0, t1 = t[:, :128], t[:, 128:]
        sq = xf * xf
        sv = (sq[:, :128] + sq[:, 128:256]) + (sq[:, 256:384] + sq[:, 384:]) - (t0 * t0 + t1 * t1)
        sm = t0 * y[:, :128] + t1 * y[:, 128:]
        for part, lines in ((sv, var), (sm, mean)):
            for b in range(4):
                lines.append(jnp.sum(part[128 * b : 128 * b + 128].T, axis=0, keepdims=True))
    return jnp.concatenate(var, axis=0), jnp.concatenate(mean, axis=0)


def group_kernel(
    n_mem, count, vox, weight, bias, ids, targets, qids, out,
    slab, taps, band, feats, blocks, sides, queries, t_hi, t_lo, tt_hi, tt_lo, tt_row,
    sem, wsem, bsend, brecv, ssend, srecv, psend, precv, lsend, lrecv, csend, crecv,
):
    g, m = lax.axis_index("grp"), lax.axis_index("mem")
    core, plane = lax.rem(g, 2), lax.div(g, 2)
    px, py = lax.rem(plane, 4), lax.div(plane, 4)
    zs = [lax.rem(m + n_mem + d, n_mem) for d in (1, -1, 2, -2, 3, -3, 4)]
    xs = [(py * 4 + lax.rem(px + s, 4)) * 2 + core for s in (1, 2, 3)]
    ys = [(lax.rem(py + s, 4) * 4 + px) * 2 + core for s in (1, 2, 3)]
    other = plane * 2 + (1 - core)

    barrier = pltpu.get_barrier_semaphore()
    for peer in [(g, z) for z in zs] + [(h, m) for h in xs + ys + [other]]:
        pl.semaphore_signal(barrier, inc=1, device_id=peer, device_id_type=MESH)

    factor = (t_hi, t_lo, tt_hi, tt_lo, tt_row)
    for ref in factor:
        ref[...] = jnp.zeros_like(ref)
    pay, aux, qrows = blocks.at[0], sides.at[0], queries.at[core, py, px]
    features(
        count, vox, weight, bias, ids, targets, qids, pay, aux, qrows, slab, taps, band, feats, sem, wsem
    )
    pl.semaphore_wait(barrier, 14)

    def remote(src, dst, send, recv, peer):
        return pltpu.make_async_remote_copy(
            src_ref=src, dst_ref=dst, send_sem=send, recv_sem=recv, device_id=peer, device_id_type=MESH
        )

    hops = []
    for i, z in enumerate(zs):
        hops.append(
            (
                remote(pay, blocks.at[i + 1], bsend.at[i], brecv.at[i], (g, z)),
                remote(aux, sides.at[i + 1], ssend.at[i], srecv.at[i], (g, z)),
            )
        )
    for codes, side in hops:
        side.start()
        codes.start()

    half = NQ // 2
    top, bottom = pl.ds(0, half), pl.ds(half, half)
    near = [
        remote(qrows.at[top], queries.at[core, py, px, top], psend.at[i], precv.at[i], (xs[i], m))
        for i in range(3)
    ] + [
        remote(
            qrows.at[bottom], queries.at[core, py, px, bottom], psend.at[3 + i], precv.at[3 + i], (ys[i], m)
        )
        for i in range(3)
    ]
    row, column = queries.at[core, py, :, top], queries.at[core, :, px, bottom]
    far = [remote(row, row, lsend.at[i], lrecv.at[i], (ys[i], m)) for i in range(3)] + [
        remote(column, column, lsend.at[3 + i], lrecv.at[3 + i], (xs[i], m)) for i in range(3)
    ]
    pieces = []
    for i, shift in enumerate((0, 1, 2, 3)):
        wy, wx = lax.rem(py + 4 - shift, 4), lax.rem(px + 4 - shift, 4)
        for j, piece in enumerate((queries.at[core, wy, :, top], queries.at[core, :, wx, bottom])):
            pieces.append(remote(piece, piece, csend.at[2 * i + j], crecv.at[2 * i + j], (other, m)))
    for copy in near:
        copy.start()

    def step(slots, at):
        for slot in slots:
            if slot > 0:
                hops[slot - 1][0].wait_recv()
                hops[slot - 1][1].wait_recv()
        lo, hi = slots[0], slots[-1] + 1
        eliminate(
            blocks[lo:hi].reshape((hi - lo) * HIT, F), [sides[i] for i in slots], at, lo == 0, *factor
        )

    step((0,), 192)
    for copy in near:
        copy.wait_recv()
    for i in (0, 3, 2, 5, 1, 4):
        far[i].start()
    for copy in pieces[:2]:
        copy.start()
    step((1, 2), 0)
    step((3, 4), 64)
    for i in (0, 2):
        for j in range(2):
            far[3 * j + i].wait_recv()
            pieces[2 * (i + 1) + j].start()
    step((5, 6), 128)
    for j in range(2):
        far[3 * j + 1].wait_recv()
        pieces[4 + j].start()
    step((7,), 224)

    def half_lines(which):
        return evaluate(queries.at[which].reshape(16, NQ, F), tt_hi, tt_lo, tt_row)

    near_half = half_lines(core)
    for copy in pieces:
        copy.wait_recv()
    far_half = half_lines(1 - core)
    for i in range(2):
        even = jnp.where(core == 0, near_half[i], far_half[i])
        odd = jnp.where(core == 0, far_half[i], near_half[i])
        for side in range(2):
            lanes = slice(NQ * side, NQ * (side + 1))
            out[i, pl.ds(side, 8, stride=2), :] = jnp.concatenate([even[:, lanes], odd[:, lanes]], axis=1)

    for codes, side in hops:
        codes.wait_send()
        side.wait_send()
    for copy in near + far + pieces:
        copy.wait_send()


def group_posterior(n_mem, count, vox, weight, bias, ids, targets, qids):
    vmem, hbm = pl.BlockSpec(memory_space=pltpu.VMEM), pl.BlockSpec(memory_space=pl.ANY)
    dma = pltpu.SemaphoreType.DMA
    return pl.pallas_call(
        functools.partial(group_kernel, n_mem),
        out_shape=jax.ShapeDtypeStruct((2, 16, 128), F32),
        in_specs=[pl.BlockSpec(memory_space=pltpu.SMEM), hbm, hbm, vmem, vmem, vmem, vmem],
        out_specs=vmem,
        scratch_shapes=[
            pltpu.VMEM((EDGE, EDGE, NP, EDGE * C), BF16),
            pltpu.VMEM((3, 3, 3, C, C), BF16),
            pltpu.VMEM((9 * EDGE * C, 4 * C), BF16),
            pltpu.VMEM((NP, F), F32),
            pltpu.VMEM((n_mem, HIT, F), jnp.int16),
            pltpu.VMEM((n_mem, 8, 128), F32),
            pltpu.VMEM((2, 4, 4, NQ, F), BF16),
            pltpu.VMEM((256, FU), BF16),
            pltpu.VMEM((256, FU), BF16),
            pltpu.VMEM((FU, 256), BF16),
            pltpu.VMEM((FU, 256), BF16),
            pltpu.VMEM((8, 256), F32),
            dma((EDGE,)), dma((1,)), dma((7,)), dma((7,)), dma((7,)), dma((7,)),
            dma((6,)), dma((6,)), dma((6,)), dma((6,)), dma((8,)), dma((8,)),
        ],
        compiler_params=pltpu.CompilerParams(
            collective_id=0, has_side_effects=True, vmem_limit_bytes=63 << 20
        ),
        name="group_posterior",
    )(count, vox, weight, bias, ids, targets, qids)


def on_device(n_mem, voxels, conv_weight, conv_bias, row_counts, sample_patch, targets, query_patch):
    out = group_posterior(
        n_mem,
        row_counts,
        voxels.transpose(1, 2, 0, 3),
        conv_weight,
        conv_bias.reshape(1, C),
        sample_patch.reshape(1, -1),
        targets.reshape(1, -1),
        query_patch.reshape(1, -1),
    )
    return out[0].reshape(1, 1, -1), out[1].reshape(1, 1, -1)


def solution(mesh):
    rows = ("grp", "mem")
    in_specs = (P(rows, None, None, None), P(), P(), P(rows), P(rows), P(rows), P(rows))
    out_specs = (P("grp", "mem", None), P("grp", "mem", None))
    return jax.shard_map(
        functools.partial(on_device, mesh.shape["mem"]),
        mesh=mesh,
        in_specs=in_specs,
        out_specs=out_specs,
        check_vma=False,
    )
```

```python
import functools

import jax
import jax.numpy as jnp
from jax import lax
from jax.experimental import pallas as pl
from jax.experimental.pallas import tpu as pltpu
from jax.sharding import PartitionSpec as P

C = 64
EDGE = 6
NP = 128
HIT = 32
F = 512
NQ = 64
FU = F + 128
TOP = 32767.0
MESH = pl.DeviceIdType.MESH
F32 = jnp.float32
BF16 = jnp.bfloat16
HIGHEST = lax.Precision.HIGHEST


def iota(shape, dim):
    return lax.broadcasted_iota(jnp.int32, shape, dim)


def split2(x):
    hi = x.astype(BF16)
    return hi, (x - hi.astype(F32)).astype(BF16)


def dot(a, b, ca=1, cb=0, precision=None):
    return lax.dot_general(
        a, b, (((ca,), (cb,)), ((), ())), precision=precision, preferred_element_type=F32
    )


def fill_band(weight, band):
    zero = jnp.zeros((C, C), BF16)
    for dx in range(3):
        for dy in range(3):
            taps = [weight[dx, dy, dz] for dz in range(3)]
            at = lambda d: taps[d] if 0 <= d <= 2 else zero
            for zi in range(EDGE):
                row = (dx * 3 + dy) * EDGE * C + zi * C
                band[row : row + C, : 2 * C] = jnp.concatenate([at(zi), at(zi - 2)], axis=1)
                band[row : row + C, 2 * C :] = jnp.concatenate([at(zi - 1), at(zi - 3)], axis=1)


def features(
    count, vox, weight, bias, ids, targets, qids, pay, aux, qrows, slab, taps, band, feats, sem, wsem
):
    copies = [pltpu.make_async_copy(vox.at[x], slab.at[x], sem.at[x]) for x in range(EDGE)]
    taps_in = pltpu.make_async_copy(weight, taps, wsem.at[0])
    taps_in.start()
    for copy in copies:
        copy.start()

    live = iota((HIT, ids.shape[1]), 1) < count[0]
    mine = jnp.logical_and(ids[...] == iota((HIT, ids.shape[1]), 0), live)
    hits = jnp.sum(jnp.where(mine, 1.0, 0.0), axis=1, keepdims=True)
    tsum = jnp.sum(jnp.where(mine, targets[...], 0.0), axis=1, keepdims=True)
    root = jnp.sqrt(hits)
    scaled = jnp.where(hits > 0, tsum / jnp.where(hits > 0, root, 1.0), 0.0)
    taps_in.wait()
    fill_band(taps, band)
    shift = jnp.concatenate([bias[...]] * 4, axis=1)
    waited = 0
    for cx in range(2):
        while waited < 2 * cx + 4:
            copies[waited].wait()
            waited += 1
        for cy in range(2):
            lhs = jnp.concatenate(
                [
                    slab[2 * cx + dx : 2 * cx + dx + 2, 2 * cy + dy : 2 * cy + dy + 2].reshape(
                        4 * NP, EDGE * C
                    )
                    for dx in range(3)
                    for dy in range(3)
                ],
                axis=1,
            )
            act = jnp.tanh(dot(lhs, band[...]) + shift).reshape(4, NP, 4 * C)
            pooled = (act[0] + act[1]) + (act[2] + act[3])
            cell = (pooled[:, : 2 * C] + pooled[:, 2 * C :]) * 0.125
            feats[:, (2 * cx + cy) * 2 * C : (2 * cx + cy + 1) * 2 * C] = cell

    rows = feats[:HIT, :]
    peak = jnp.max(jnp.abs(rows), axis=1, keepdims=True)
    unit = jnp.where(peak > 0, TOP / jnp.where(peak > 0, peak, 1.0), 0.0)
    pay[...] = jnp.round(rows * unit).astype(jnp.int32).astype(jnp.int16)
    lane = iota((HIT, 128), 1)
    sides = jnp.where(lane == 0, scaled, jnp.where(lane == 1, peak * (root * (1.0 / TOP)), 0.0))
    aux[...] = jnp.concatenate([sides.T[:8, :], jnp.zeros((8, 128 - HIT), F32)], axis=1)
    pick = (iota((NP, NQ), 0) == qids[...]).astype(F32).astype(BF16)
    qrows[...] = dot(pick, feats[...].astype(BF16), 0, 0).astype(BF16)


def spread(x, shape=(8, 128)):
    return jnp.broadcast_to(x, shape)


def inverse_factor(gram):
    n = gram.shape[0]
    eye = jnp.where(iota((n, n), 0) == iota((n, n), 1), 1.0, 0.0)
    parts = [gram, eye] if n == 64 else [gram, eye, jnp.zeros((n, 128 - 2 * n), F32)]
    wide = jnp.concatenate(parts, axis=1)
    sub = iota((8, 128), 0)
    count = n // 8
    rows = [wide[8 * b : 8 * b + 8] for b in range(count)]

    def columns(t, b):
        return [spread(rows[t][:, 8 * b + c : 8 * b + c + 1]) for c in range(8)]

    done = []
    diagonal = columns(0, 0)
    for b in range(count):
        cols = {t: columns(t, b) for t in range(b + 1, count)}
        cols[b] = diagonal
        ahead = b + 1 < count
        if ahead:
            coming, taken = columns(b + 1, b + 1), [None] * 8
        for j in range(8):
            heads = [spread(cols[b][c][j : j + 1, :]) for c in range(j, 8)]
            inv = 1.0 / heads[0]
            times = {
                t: (jnp.where(sub > j, cols[t][j], 0.0) if t == b else cols[t][j]) * inv
                for t in range(b, count)
            }
            row = spread(rows[b][j : j + 1, :])
            for t in range(b, count):
                for c in range(j + 1, 8):
                    cols[t][c] = cols[t][c] - times[t] * heads[c - j]
            for t in range(b, count):
                rows[t] = rows[t] - times[t] * row
            if ahead:
                for c in range(8):
                    term = times[b + 1] * spread(cols[b + 1][j][c : c + 1, :])
                    taken[c] = term if taken[c] is None else taken[c] + term
        pivots = cols[b][0]
        for j in range(1, 8):
            pivots = jnp.where(sub == j, cols[b][j], pivots)
        done.append(rows[b] * lax.rsqrt(pivots))
        if ahead:
            diagonal = [coming[c] - taken[c] for c in range(8)]
    return jnp.concatenate(done, axis=0)[:, n : 2 * n]


def eliminate(codes, sides, at, first, t_hi, t_lo, tt_hi, tt_lo, tt_row):
    n = codes.shape[0]
    column = jnp.concatenate([side.T[:HIT] for side in sides], axis=0)
    a_hi, a_lo = split2(codes.astype(jnp.int32).astype(F32) * column[:, 1:2])
    rest = jnp.concatenate(
        [
            a_hi.astype(F32) + a_lo.astype(F32),
            jnp.where(iota((n, 128), 1) == 0, column[:, 0:1], 0.0),
        ],
        axis=1,
    )
    both = jnp.concatenate([a_hi, a_lo], axis=0)
    gg = dot(both, both, 1, 1)
    gram = gg[:n, :n] + (gg[:n, n:] + gg[n:, :n])
    gram = gram + jnp.where(iota((n, n), 0) == iota((n, n), 1), 8.0, 0.0)
    if not first:
        part = dot(both, tt_hi[:F, :])
        low = part[:n] + (part[n:] + dot(a_hi, tt_lo[:F, :]))
        gram = gram - dot(low, low, 1, 1, HIGHEST)
        l_hi, l_lo = split2(low)
        part = dot(jnp.concatenate([l_hi, l_lo], axis=0), t_hi[...])
        rest = rest - (part[:n] + (part[n:] + dot(l_hi, t_lo[...])))
    i_hi, i_lo = split2(inverse_factor(gram))
    b_hi, b_lo = split2(rest)
    part = dot(jnp.concatenate([i_hi, i_lo], axis=0), b_hi)
    rows = part[:n] + (part[n:] + dot(i_hi, b_lo))
    r_hi, r_lo = split2(rows)
    t_hi[at : at + n, :] = r_hi
    t_lo[at : at + n, :] = r_lo
    cols = rows.T
    c_hi, c_lo = split2(cols)
    tt_hi[:, at : at + n] = c_hi
    tt_lo[:, at : at + n] = c_lo
    tt_row[:, at : at + n] = cols[F : F + 8, :]


def evaluate(queries, tt_hi, tt_lo, tt_row):
    y = tt_row[0:1, :]
    var, mean = [], []
    for i in range(2):
        x = queries[8 * i : 8 * i + 8].reshape(8 * NQ, F)
        t = dot(x, tt_hi[:F, :]) + dot(x, tt_lo[:F, :])
        xf = x.astype(F32)
        t0, t1 = t[:, :128], t[:, 128:]
        sq = xf * xf
        sv = (sq[:, :128] + sq[:, 128:256]) + (sq[:, 256:384] + sq[:, 384:]) - (t0 * t0 + t1 * t1)
        sm = t0 * y[:, :128] + t1 * y[:, 128:]
        for part, lines in ((sv, var), (sm, mean)):
            for b in range(4):
                lines.append(jnp.sum(part[128 * b : 128 * b + 128].T, axis=0, keepdims=True))
    return jnp.concatenate(var, axis=0), jnp.concatenate(mean, axis=0)


def group_kernel(
    n_mem, count, vox, weight, bias, ids, targets, qids, out,
    slab, taps, band, feats, blocks, sides, queries, t_hi, t_lo, tt_hi, tt_lo, tt_row,
    sem, wsem, bsend, brecv, ssend, srecv, psend, precv, lsend, lrecv, csend, crecv,
):
    g, m = lax.axis_index("grp"), lax.axis_index("mem")
    core, plane = lax.rem(g, 2), lax.div(g, 2)
    px, py = lax.rem(plane, 4), lax.div(plane, 4)
    zs = [lax.rem(m + n_mem + d, n_mem) for d in (1, -1, 2, -2, 3, -3, 4)]
    xs = [(py * 4 + lax.rem(px + s, 4)) * 2 + core for s in (1, 2, 3)]
    ys = [(lax.rem(py + s, 4) * 4 + px) * 2 + core for s in (1, 2, 3)]
    other = plane * 2 + (1 - core)

    barrier = pltpu.get_barrier_semaphore()
    for peer in [(g, z) for z in zs] + [(h, m) for h in xs + ys + [other]]:
        pl.semaphore_signal(barrier, inc=1, device_id=peer, device_id_type=MESH)

    factor = (t_hi, t_lo, tt_hi, tt_lo, tt_row)
    for ref in factor:
        ref[...] = jnp.zeros_like(ref)
    pay, aux, qrows = blocks.at[0], sides.at[0], queries.at[core, py, px]
    features(
        count, vox, weight, bias, ids, targets, qids, pay, aux, qrows, slab, taps, band, feats, sem, wsem
    )
    pl.semaphore_wait(barrier, 14)

    def remote(src, dst, send, recv, peer):
        return pltpu.make_async_remote_copy(
            src_ref=src, dst_ref=dst, send_sem=send, recv_sem=recv, device_id=peer, device_id_type=MESH
        )

    hops = []
    for i, z in enumerate(zs):
        hops.append(
            (
                remote(pay, blocks.at[i + 1], bsend.at[i], brecv.at[i], (g, z)),
                remote(aux, sides.at[i + 1], ssend.at[i], srecv.at[i], (g, z)),
            )
        )
    half = NQ // 2
    top, bottom = pl.ds(0, half), pl.ds(half, half)
    near = [
        remote(qrows.at[top], queries.at[core, py, px, top], psend.at[i], precv.at[i], (xs[i], m))
        for i in range(3)
    ] + [
        remote(
            qrows.at[bottom], queries.at[core, py, px, bottom], psend.at[3 + i], precv.at[3 + i], (ys[i], m)
        )
        for i in range(3)
    ]
    row, column = queries.at[core, py, :, top], queries.at[core, :, px, bottom]
    far = [remote(row, row, lsend.at[i], lrecv.at[i], (ys[i], m)) for i in range(3)] + [
        remote(column, column, lsend.at[3 + i], lrecv.at[3 + i], (xs[i], m)) for i in range(3)
    ]
    pieces = []
    for i, shift in enumerate((0, 1, 2, 3)):
        wy, wx = lax.rem(py + 4 - shift, 4), lax.rem(px + 4 - shift, 4)
        for j, piece in enumerate((queries.at[core, wy, :, top], queries.at[core, :, wx, bottom])):
            pieces.append(remote(piece, piece, csend.at[2 * i + j], crecv.at[2 * i + j], (other, m)))
    for copy in near:
        copy.start()

    for codes, side in hops:
        side.start()
        codes.start()

    def step(slots, at):
        for slot in slots:
            if slot > 0:
                hops[slot - 1][0].wait_recv()
                hops[slot - 1][1].wait_recv()
        lo, hi = slots[0], slots[-1] + 1
        eliminate(
            blocks[lo:hi].reshape((hi - lo) * HIT, F), [sides[i] for i in slots], at, lo == 0, *factor
        )

    step((0,), 192)
    for copy in near:
        copy.wait_recv()
    for i in (0, 3, 2, 5, 1, 4):
        far[i].start()
    for copy in pieces[:2]:
        copy.start()
    step((1, 2), 0)
    step((3, 4), 64)
    for i in (0, 2):
        for j in range(2):
            far[3 * j + i].wait_recv()
            pieces[2 * (i + 1) + j].start()
    step((5, 6), 128)
    for j in range(2):
        far[3 * j + 1].wait_recv()
        pieces[4 + j].start()
    step((7,), 224)

    def half_lines(which):
        return evaluate(queries.at[which].reshape(16, NQ, F), tt_hi, tt_lo, tt_row)

    near_half = half_lines(core)
    for copy in pieces:
        copy.wait_recv()
    far_half = half_lines(1 - core)
    for i in range(2):
        even = jnp.where(core == 0, near_half[i], far_half[i])
        odd = jnp.where(core == 0, far_half[i], near_half[i])
        for side in range(2):
            lanes = slice(NQ * side, NQ * (side + 1))
            out[i, pl.ds(side, 8, stride=2), :] = jnp.concatenate([even[:, lanes], odd[:, lanes]], axis=1)

    for codes, side in hops:
        codes.wait_send()
        side.wait_send()
    for copy in near + far + pieces:
        copy.wait_send()


def group_posterior(n_mem, count, vox, weight, bias, ids, targets, qids):
    vmem, hbm = pl.BlockSpec(memory_space=pltpu.VMEM), pl.BlockSpec(memory_space=pl.ANY)
    dma = pltpu.SemaphoreType.DMA
    return pl.pallas_call(
        functools.partial(group_kernel, n_mem),
        out_shape=jax.ShapeDtypeStruct((2, 16, 128), F32),
        in_specs=[pl.BlockSpec(memory_space=pltpu.SMEM), hbm, hbm, vmem, vmem, vmem, vmem],
        out_specs=vmem,
        scratch_shapes=[
            pltpu.VMEM((EDGE, EDGE, NP, EDGE * C), BF16),
            pltpu.VMEM((3, 3, 3, C, C), BF16),
            pltpu.VMEM((9 * EDGE * C, 4 * C), BF16),
            pltpu.VMEM((NP, F), F32),
            pltpu.VMEM((n_mem, HIT, F), jnp.int16),
            pltpu.VMEM((n_mem, 8, 128), F32),
            pltpu.VMEM((2, 4, 4, NQ, F), BF16),
            pltpu.VMEM((256, FU), BF16),
            pltpu.VMEM((256, FU), BF16),
            pltpu.VMEM((FU, 256), BF16),
            pltpu.VMEM((FU, 256), BF16),
            pltpu.VMEM((8, 256), F32),
            dma((EDGE,)), dma((1,)), dma((7,)), dma((7,)), dma((7,)), dma((7,)),
            dma((6,)), dma((6,)), dma((6,)), dma((6,)), dma((8,)), dma((8,)),
        ],
        compiler_params=pltpu.CompilerParams(
            collective_id=0, has_side_effects=True, vmem_limit_bytes=63 << 20
        ),
        name="group_posterior",
    )(count, vox, weight, bias, ids, targets, qids)


def on_device(n_mem, voxels, conv_weight, conv_bias, row_counts, sample_patch, targets, query_patch):
    out = group_posterior(
        n_mem,
        row_counts,
        voxels.transpose(1, 2, 0, 3),
        conv_weight,
        conv_bias.reshape(1, C),
        sample_patch.reshape(1, -1),
        targets.reshape(1, -1),
        query_patch.reshape(1, -1),
    )
    return out[0].reshape(1, 1, -1), out[1].reshape(1, 1, -1)


def solution(mesh):
    rows = ("grp", "mem")
    in_specs = (P(rows, None, None, None), P(), P(), P(rows), P(rows), P(rows), P(rows))
    out_specs = (P("grp", "mem", None), P("grp", "mem", None))
    return jax.shard_map(
        functools.partial(on_device, mesh.shape["mem"]),
        mesh=mesh,
        in_specs=in_specs,
        out_specs=out_specs,
        check_vma=False,
    )
```
